256 devices in a mesh: seq: 64 (over x_lo, z, y), head: 4 (over x_hi, core).
Axes of the slice: x: 4 (x_hi: 2, x_lo: 2; x = x_hi * 2 + x_lo), y: 4, z: 8, core: 2. Of those that a mesh axis runs over, the one named last changes fastest.
Arguments:
- tokens: bfloat16 [32768, 2048], P(('seq', 'head'))
- ln_gain: float32 [2048], replicated, may hold values from 0.1 to 1.9
- w_qkv: bfloat16 [2048, 3, 2048], P(None, None, 'head')
- slopes: float32 [16], P('head')
- w_out: bfloat16 [2048, 2048], P('head'), may hold values from -0.125 to 0.125
- seg_ids: int32 [32768], P('seq'), may hold values from 0 to 31, never falling along the last dimension, each value on 1 to 2048 neighbouring positions
Outputs:
- hidden: bfloat16 [32768, 2048], P(('seq', 'head'))
- key_cache: bfloat16 [32768, 2048], P('seq', 'head')
- value_cache: bfloat16 [32768, 2048], P('seq', 'head')
The draws below stay inside these ranges and needn't reach their ends.
Inputs may be any that keep to these rules, and one draw needn't show every extreme that they name: `seg_ids`: Non-decreasing along the stream; each prompt number names 1 to 2048 consecutive tokens, one prompt exactly 2048.
All inputs are finite; a program needn't handle non-finite values.
Results may differ from the reference program's by a relative error of at most 0.0075.
Values may be sent and summed in bfloat16 or wider, within the bound.
A program may use at most 128 MiB of HBM per device.

```python
import math
import jax
import jax.numpy as jnp
import numpy as np
from jax import lax

D = 2048
HEADS = 16
HD = 128
TOK_DEV = 512
SPAN = 4
HEADS_DEV = 4
TOKENS = 32768
SEG_MOST = 2048
PROMPTS = 32
N_SEQ = 64
N_HEAD = 4


def draw_tokens(key, part):
    k_rough = jax.random.fold_in(key, 31)
    k_period = jax.random.fold_in(key, 32)
    k_phase = jax.random.fold_in(key, 33)
    positions = jnp.arange(TOKENS, dtype=jnp.float32)[:, None]
    periods = jnp.exp(jax.random.uniform(k_period, (1, D), jnp.float32, math.log(300.0), math.log(6000.0)))
    phases = jax.random.uniform(k_phase, (1, D), jnp.float32, -math.pi, math.pi)
    smooth = jnp.sin(2.0 * math.pi * positions / periods + phases)
    values = jax.random.normal(k_rough, (TOKENS, D), jnp.float32) + smooth
    return values.astype(jnp.bfloat16)


def draw_w_qkv(key, part):
    base = jax.random.normal(jax.random.fold_in(key, 41), (D, 3, HEADS * HD), jnp.float32) * D ** (-0.5)
    values = base
    return values.astype(jnp.bfloat16)


def draw_slopes(key, part):
    values = jnp.exp(jax.random.uniform(jax.random.fold_in(key, 51), (HEADS,), jnp.float32, math.log(0.0002), math.log(0.4)))
    return values.astype(jnp.float32)


def levels(key, shape, pieces, smallest, largest):
    factor_of = 1.0
    for dim, parts in pieces:
        draws = jax.random.uniform(jax.random.fold_in(jax.random.fold_in(key, 6), dim), (parts,), jnp.float32, smallest / len(pieces), largest / len(pieces))
        factor_of = factor_of * jnp.repeat(jnp.exp(draws), shape[dim] // parts).reshape((-1,) + (1,) * (len(shape) - 1 - dim))
    return factor_of


def split_up(number_of, total, limit, lean):
    loads = [(1 << 20) // math.isqrt(grade ** lean) + 1 for grade in range(2, number_of + 1)]
    rest, given = total - limit - (number_of - 1), [1] * (number_of - 1)
    while rest > 0:
        free = [i for i in range(number_of - 1) if given[i] < limit]
        pool, budget = sum([loads[i] for i in free]), rest
        for i in free:
            more = min(limit - given[i], max(1, budget * loads[i] // pool), rest)
            given[i] = given[i] + more
            rest = rest - more
    return np.array([limit] + given)


def ragged(rng, amount, total, bound, slope):
    if amount == 2:
        one = jax.random.randint(rng, (), max(1, total - bound), min(bound, total - 1) + 1)
        return jnp.stack([one, total - one])
    sizes = jnp.asarray(split_up(amount, total, bound, slope), jnp.int32)
    twos = (amount - 1) // 2
    donor, sink = sizes[1:1 + 2 * twos:2], sizes[2:2 + 2 * twos:2]
    slack = jnp.minimum(donor - 1, bound - sink)
    passed = jax.random.randint(jax.random.fold_in(rng, 1), (twos,), 0, 1 << 20) % (slack + 1)
    sizes = sizes.at[1:1 + 2 * twos:2].set(donor - passed).at[2:2 + 2 * twos:2].set(sink + passed)
    return sizes[jax.random.permutation(jax.random.fold_in(rng, 2), amount)]


def noise(rng, shape, scale, limit, cuts=(), kind=jnp.bfloat16):
    result = scale * jax.random.normal(rng, shape, jnp.float32)
    if cuts:
        result = result * levels(rng, shape, cuts, -0.22, 0.18)
    return jnp.clip(result, -limit, limit).astype(kind)


def setup_inputs(seed: int = 0) -> dict:
    arg_keys = jax.random.split(jax.random.key(seed), 7)
    return {
        "tokens": draw_tokens(jax.random.fold_in(arg_keys[6], 71), 0),
        "ln_gain": jnp.clip(1.0 + 0.18 * jax.random.normal(arg_keys[1], (D,), jnp.float32), 0.1, 1.9),
        "w_qkv": draw_w_qkv(jax.random.fold_in(arg_keys[6], 71), 0),
        "slopes": draw_slopes(jax.random.fold_in(arg_keys[6], 71), 0),
        "w_out": noise(arg_keys[4], (HEADS * HD, D), (HEADS * HD) ** -0.5, 0.125, ((0, 4),)),
        "seg_ids": jnp.searchsorted(jnp.cumsum(ragged(arg_keys[5], PROMPTS, TOKENS, SEG_MOST, 2)), jnp.arange(TOKENS), side="right").astype(jnp.int32),
    }


EPSILON = 1e-05
NEG_FILL = -1e+30

def attend_block(block_num, query, key_pad, value_pad, seg_pad, seg_ids, slopes):
    first = (block_num * TOK_DEV).astype(jnp.int32)
    reach = (SPAN + 1) * TOK_DEV
    q_block = lax.dynamic_slice_in_dim(query, first, TOK_DEV, 0).reshape(TOK_DEV, HEADS, HD).astype(jnp.float32)
    k_block = lax.dynamic_slice_in_dim(key_pad, first, reach, 0).reshape(reach, HEADS, HD).astype(jnp.float32)
    v_block = lax.dynamic_slice_in_dim(value_pad, first, reach, 0).reshape(reach, HEADS, HD).astype(jnp.float32)
    seg_key = lax.dynamic_slice_in_dim(seg_pad, first, reach, 0)
    seg_query = lax.dynamic_slice_in_dim(seg_ids, first, TOK_DEV, 0)
    q_pos = first + jnp.arange(TOK_DEV, dtype=jnp.int32)
    k_pos = first - SPAN * TOK_DEV + jnp.arange(reach, dtype=jnp.int32)
    scores = jnp.einsum('qhe,khe->qhk', q_block, k_block) * HD ** (-0.5)
    distance = (q_pos[:, None] - k_pos[None, :]).astype(jnp.float32)
    scores = scores - slopes.astype(jnp.float32)[None, :, None] * distance[:, None, :]
    valid_mask = ((seg_query[:, None] == seg_key[None, :]) & (k_pos[None, :] <= q_pos[:, None]) & (k_pos[None, :] >= 0))[:, None, :]
    scores = jnp.where(valid_mask, scores, NEG_FILL)
    row_max = lax.optimization_barrier(jnp.max(scores, axis=-1, keepdims=True))
    expo = jnp.where(valid_mask, jnp.exp(scores - row_max), 0.0)
    denominator = lax.optimization_barrier(jnp.sum(expo, axis=-1))
    probs = lax.optimization_barrier(expo.astype(jnp.bfloat16)).astype(jnp.float32)
    context = jnp.einsum('qhk,khe->qhe', probs, v_block) / denominator[..., None]
    return context.astype(jnp.bfloat16).reshape(TOK_DEV, HEADS * HD)

def reference(tokens, ln_gain, w_qkv, slopes, w_out, seg_ids):
    inputs = tokens.astype(jnp.float32)
    row_mean = lax.optimization_barrier(jnp.mean(inputs, axis=-1, keepdims=True))
    centred = inputs - row_mean
    variance = lax.optimization_barrier(jnp.mean(centred * centred, axis=-1, keepdims=True))
    normed = (centred * lax.rsqrt(variance + EPSILON) * ln_gain.astype(jnp.float32)).astype(jnp.bfloat16)
    width = HEADS * HD
    qkv_rows = jnp.dot(normed, w_qkv.reshape(D, 3 * width), preferred_element_type=jnp.float32).astype(jnp.bfloat16)
    query = qkv_rows[:, :width]
    key_cache = qkv_rows[:, width:2 * width]
    value_cache = qkv_rows[:, 2 * width:]
    key_pad = jnp.concatenate([jnp.zeros((SPAN * TOK_DEV, width), jnp.bfloat16), key_cache], axis=0)
    value_pad = jnp.concatenate([jnp.zeros((SPAN * TOK_DEV, width), jnp.bfloat16), value_cache], axis=0)
    seg_pad = jnp.concatenate([jnp.full((SPAN * TOK_DEV,), -1, jnp.int32), seg_ids.astype(jnp.int32)], axis=0)
    context = lax.map(lambda block_num: attend_block(block_num, query, key_pad, value_pad, seg_pad, seg_ids.astype(jnp.int32), slopes), jnp.arange(N_SEQ, dtype=jnp.int32))
    context = context.reshape(TOKENS, width)
    group_cols = HEADS_DEV * HD
    summed = inputs
    for group in range(N_HEAD):
        partial_g = jnp.dot(context[:, group * group_cols:(group + 1) * group_cols], w_out[group * group_cols:(group + 1) * group_cols, :], preferred_element_type=jnp.float32)
        summed = summed + lax.optimization_barrier(partial_g.astype(jnp.bfloat16)).astype(jnp.float32)
    return (summed.astype(jnp.bfloat16), key_cache, value_cache)
```

```python
import jax
import jax.numpy as jnp
from jax import lax
from jax.sharding import PartitionSpec as P

HD = 128
SPAN = 4


EPSILON = 1e-05
NEG_FILL = -1e30


def shifted(value, axis, steps):
    count = lax.axis_size(axis)
    leading, last = (max(0, -steps), min(count, count - steps))
    return lax.ppermute(value, axis, [(source, source + steps) for source in range(leading, last)])


def swapped(value, axis, mask):
    count = lax.axis_size(axis)
    return lax.ppermute(value, axis, [(source, source ^ mask) for source in range(count)])


def layer_norm(inputs, ln_gain):
    row_mean = jnp.mean(inputs, axis=-1, keepdims=True)
    centred = inputs - row_mean
    variance = jnp.mean(centred * centred, axis=-1, keepdims=True)
    return (centred * lax.rsqrt(variance + EPSILON) * ln_gain).astype(jnp.bfloat16)


def attend_one(run_state, queries, q_pos, seg_query, slopes_dev, keys, values, seg_key, k_pos):
    prev_max, prev_sum, prev_acc = run_state
    scores = jnp.einsum(
        "hqe,hke->hqk", queries, keys, preferred_element_type=jnp.float32
    ) * HD ** (-0.5)
    distance = (q_pos[:, None] - k_pos[None, :]).astype(jnp.float32)
    scores = scores - slopes_dev[:, None, None] * distance[None, :, :]
    valid_mask = (
        (seg_query[:, None] == seg_key[None, :])
        & (k_pos[None, :] <= q_pos[:, None])
        & (k_pos[None, :] >= 0)
    )[None, :, :]
    scores = jnp.where(valid_mask, scores, NEG_FILL)
    row_max = jnp.maximum(prev_max, jnp.max(scores, axis=-1))
    expo = jnp.where(valid_mask, jnp.exp(scores - row_max[..., None]), 0.0)
    rescale = jnp.exp(prev_max - row_max)
    new_sum = prev_sum * rescale + jnp.sum(expo, axis=-1)
    new_acc = prev_acc * rescale[..., None] + jnp.einsum(
        "hqk,hke->hqe", expo.astype(jnp.bfloat16), values, preferred_element_type=jnp.float32
    )
    return (row_max, new_sum, new_acc)


def on_device(tokens, ln_gain, w_qkv, slopes, w_out, seg_ids):
    inputs = tokens.astype(jnp.float32)
    normed = layer_norm(inputs, ln_gain)
    rows_dev = normed.shape[0]
    head = lax.axis_index("head")
    n_head = lax.axis_size("head")

    cross = swapped(normed, "head", 2)
    partner = swapped(jnp.stack([normed, cross]), "head", 1)
    pieces = jnp.stack([normed, partner[0], cross, partner[1]])
    order = jnp.arange(n_head, dtype=jnp.int32) ^ head
    block_rows = jnp.take(pieces, order, axis=0).reshape(n_head * rows_dev, normed.shape[1])

    width_local = w_qkv.shape[2]
    heads_dev = slopes.shape[0]
    joined = w_qkv.reshape(w_qkv.shape[0], 3 * width_local)
    qkv_rows = jnp.dot(block_rows, joined, preferred_element_type=jnp.float32).astype(jnp.bfloat16)
    block_len = qkv_rows.shape[0]
    key_cache = qkv_rows[:, width_local : 2 * width_local]
    value_cache = qkv_rows[:, 2 * width_local :]

    def head_major(cols):
        return cols.reshape(block_len, heads_dev, HD).transpose(1, 0, 2)

    queries = head_major(qkv_rows[:, :width_local])
    keys_hm = head_major(key_cache)
    values_hm = head_major(value_cache)

    seg_rows = seg_ids.astype(jnp.bfloat16).reshape(block_len // HD, HD)
    pad_rows = (-seg_rows.shape[0]) % 8
    seg_rows = jnp.concatenate([seg_rows, jnp.zeros((pad_rows, HD), jnp.bfloat16)], axis=0)
    kv_len = heads_dev * block_len
    payload = jnp.concatenate(
        [keys_hm.reshape(kv_len, HD), values_hm.reshape(kv_len, HD), seg_rows], axis=0
    )
    arrived = [shifted(payload, "seq", steps) for steps in range(1, SPAN + 1)]

    seq_index = lax.axis_index("seq")
    offsets = jnp.arange(block_len, dtype=jnp.int32)
    q_pos = seq_index * block_len + offsets

    initial = (
        jnp.full((heads_dev, block_len), NEG_FILL, jnp.float32),
        jnp.zeros((heads_dev, block_len), jnp.float32),
        jnp.zeros((heads_dev, block_len, HD), jnp.float32),
    )
    run_state = attend_one(
        initial, queries, q_pos, seg_ids, slopes, keys_hm, values_hm, seg_ids, q_pos
    )
    for steps_back in range(1, SPAN + 1):
        got = arrived[steps_back - 1]
        k_pos = (seq_index - steps_back) * block_len + offsets
        keys_in = got[:kv_len].reshape(heads_dev, block_len, HD)
        values_in = got[kv_len : 2 * kv_len].reshape(heads_dev, block_len, HD)
        seg_in = got[2 * kv_len : 2 * kv_len + block_len // HD].reshape(block_len).astype(jnp.int32)
        run_state = attend_one(
            run_state, queries, q_pos, seg_ids, slopes, keys_in, values_in, seg_in, k_pos
        )
    context = (run_state[2] / run_state[1][..., None]).astype(jnp.bfloat16)
    partial = jnp.einsum(
        "hqe,hed->qd",
        context,
        w_out.reshape(heads_dev, HD, w_out.shape[1]),
        preferred_element_type=jnp.float32,
    ).astype(jnp.bfloat16)

    partial4 = partial.reshape(n_head, rows_dev, partial.shape[1])
    sent = jnp.take(partial4, jnp.stack([head ^ 1, head ^ 3]), axis=0)
    kept = jnp.take(partial4, jnp.stack([head, head ^ 2]), axis=0)
    chip_sum = kept.astype(jnp.float32) + swapped(sent, "head", 1).astype(jnp.float32)
    other_chip = swapped(chip_sum[1].astype(jnp.bfloat16), "head", 2).astype(jnp.float32)
    hidden = (inputs + chip_sum[0] + other_chip).astype(jnp.bfloat16)
    return (hidden, key_cache, value_cache)


def solution(mesh):
    in_specs = (
        P(("seq", "head"), None),
        P(),
        P(None, None, "head"),
        P("head"),
        P("head", None),
        P("seq"),
    )
    out_specs = (P(("seq", "head"), None), P("seq", "head"), P("seq", "head"))
    return jax.shard_map(
        on_device, mesh=mesh, in_specs=in_specs, out_specs=out_specs, check_vma=False
    )
```

```python
import jax
import jax.numpy as jnp
from jax import lax
from jax.sharding import PartitionSpec as P
from jax.experimental import pallas as pl
from jax.experimental.pallas import tpu as pltpu

HD = 128
SPAN = 4


EPSILON = 1e-05
NEG_FILL = -1e30


def shifted(value, axis, steps):
    count = lax.axis_size(axis)
    leading, last = (max(0, -steps), min(count, count - steps))
    return lax.ppermute(value, axis, [(source, source + steps) for source in range(leading, last)])


def swapped(value, axis, mask):
    count = lax.axis_size(axis)
    return lax.ppermute(value, axis, [(source, source ^ mask) for source in range(count)])


def layer_norm(inputs, ln_gain):
    row_mean = jnp.mean(inputs, axis=-1, keepdims=True)
    centred = inputs - row_mean
    variance = jnp.mean(centred * centred, axis=-1, keepdims=True)
    return (centred * lax.rsqrt(variance + EPSILON) * ln_gain).astype(jnp.bfloat16)


TQ = 256
TK = 256


def attention_kernel(flags_ref, q_ref, *refs):
    span = len(refs) - 8
    kvs = refs[: span + 1]
    segq_ref, segk_ref, bias_ref, o_ref, m_sc, l_sc, acc_sc = refs[span + 1 :]
    heads = m_sc.shape[0]
    block_len = q_ref.shape[0]
    n_q = block_len // TQ
    n_t = block_len // TK
    width = heads * HD
    scale = HD ** (-0.5)
    for qt in range(n_q):
        m_sc[...] = jnp.full(m_sc.shape, NEG_FILL, jnp.float32)
        l_sc[...] = jnp.zeros(l_sc.shape, jnp.float32)
        acc_sc[...] = jnp.zeros(acc_sc.shape, jnp.float32)
        segq = segq_ref[pl.ds(qt * TQ, TQ), :]
        steps = [(0, qt)] + [(0, t) for t in range(n_t) if t * TK < qt * TQ]
        steps += [(blk, t) for blk in range(1, span + 1) for t in range(n_t)]
        for blk, t in steps:
            diag = blk == 0 and t == qt

            def body(blk=blk, t=t, diag=diag):
                segk = segk_ref[pl.ds(blk, 1), pl.ds(t * TK, TK)]
                valid = segq == segk
                if diag:
                    rows = lax.broadcasted_iota(jnp.int32, (TQ, TK), 0)
                    cols = lax.broadcasted_iota(jnp.int32, (TQ, TK), 1)
                    valid = valid & (cols <= rows)
                def one_head(h, carry):
                    lanes = pl.multiple_of(h * HD, HD)
                    q = q_ref[pl.ds(qt * TQ, TQ), pl.ds(lanes, HD)]
                    k = kvs[blk][pl.ds(t * TK, TK), pl.ds(lanes, HD)]
                    v = kvs[blk][pl.ds(t * TK, TK), pl.ds(width + lanes, HD)]
                    s = lax.dot_general(
                        q, k, (((1,), (1,)), ((), ())), preferred_element_type=jnp.float32
                    )
                    s = s * scale + bias_ref[pl.ds(h, 1), pl.ds(blk * block_len + t * TK, TK)]
                    s = jnp.where(valid, s, NEG_FILL)
                    m_prev = m_sc[h]
                    m_new = jnp.maximum(m_prev, jnp.max(s, axis=1, keepdims=True))
                    p = jnp.exp(s - m_new)
                    rescale = jnp.exp(m_prev - m_new)
                    l_sc[h] = l_sc[h] * rescale + jnp.sum(p, axis=1, keepdims=True)
                    acc_sc[h] = acc_sc[h] * rescale + jnp.dot(
                        p.astype(jnp.bfloat16), v, preferred_element_type=jnp.float32
                    )
                    m_sc[h] = m_new
                    return carry

                lax.fori_loop(0, heads, one_head, 0)

            if diag:
                body()
            else:
                pl.when(flags_ref[qt * (span + 1) * n_t + blk * n_t + t] != 0)(body)
        for h in range(heads):
            o_ref[pl.ds(qt * TQ, TQ), pl.ds(h * HD, HD)] = (acc_sc[h] / l_sc[h]).astype(o_ref.dtype)


def attention(queries, kv_blocks, seg_q, seg_k, slopes):
    block_len, width = queries.shape
    heads = width // HD
    span = len(kv_blocks) - 1
    n_q, n_t = block_len // TQ, block_len // TK
    offsets = jnp.arange(block_len, dtype=jnp.int32)
    rel = (jnp.arange(span + 1, dtype=jnp.int32)[:, None] * -block_len + offsets[None, :]).reshape(-1)
    bias = slopes[:, None] * rel.astype(jnp.float32)[None, :]
    seg_first = seg_q.reshape(n_q, TQ)[:, 0]
    seg_last = seg_k.reshape(span + 1, n_t, TK)[:, :, -1]
    flags = (seg_last[None, :, :] >= seg_first[:, None, None]).astype(jnp.int32).reshape(-1)
    seg_rows = jnp.concatenate(
        [seg_k, jnp.full(((-seg_k.shape[0]) % 8, block_len), -1, jnp.int32)], axis=0
    )
    vmem = pl.BlockSpec(memory_space=pltpu.VMEM)
    work = heads * block_len * (span + 1) * block_len
    return pl.pallas_call(
        attention_kernel,
        out_shape=jax.ShapeDtypeStruct((block_len, width), jnp.bfloat16),
        in_specs=[pl.BlockSpec(memory_space=pltpu.SMEM)] + [vmem] * (span + 5),
        out_specs=vmem,
        scratch_shapes=[
            pltpu.VMEM((heads, TQ, 1), jnp.float32),
            pltpu.VMEM((heads, TQ, 1), jnp.float32),
            pltpu.VMEM((heads, TQ, HD), jnp.float32),
        ],
        cost_estimate=pl.CostEstimate(
            flops=4 * work * HD, transcendentals=work, bytes_accessed=(span + 2) * block_len * width * 4
        ),
    )(flags, queries, *kv_blocks, seg_q.reshape(block_len, 1), seg_rows, bias)


def on_device(tokens, ln_gain, w_qkv, slopes, w_out, seg_ids):
    seg_all = lax.all_gather(seg_ids, "seq", axis=0, tiled=True)
    inputs = tokens.astype(jnp.float32)
    normed = layer_norm(inputs, ln_gain)
    rows_dev = normed.shape[0]
    head = lax.axis_index("head")
    n_head = lax.axis_size("head")

    cross = swapped(normed, "head", 2)
    partner = swapped(jnp.stack([normed, cross]), "head", 1)
    pieces = jnp.stack([normed, partner[0], cross, partner[1]])
    order = jnp.arange(n_head, dtype=jnp.int32) ^ head
    block_rows = jnp.take(pieces, order, axis=0).reshape(n_head * rows_dev, normed.shape[1])

    width_local = w_qkv.shape[2]
    heads_dev = slopes.shape[0]
    joined = w_qkv.reshape(w_qkv.shape[0], 3 * width_local)
    qkv_rows = jnp.dot(block_rows, joined, preferred_element_type=jnp.float32).astype(jnp.bfloat16)
    block_len = qkv_rows.shape[0]
    key_cache = qkv_rows[:, width_local : 2 * width_local]
    value_cache = qkv_rows[:, 2 * width_local :]

    kv_own = qkv_rows[:, width_local:]
    arrived = [shifted(kv_own, "seq", steps) for steps in range(1, SPAN + 1)]

    seq_index = lax.axis_index("seq")
    reach = SPAN * block_len
    seg_padded = jnp.concatenate([jnp.full((reach,), -1, jnp.int32), seg_all])
    window = lax.dynamic_slice_in_dim(seg_padded, seq_index * block_len, reach + block_len)
    seg_k = window.reshape(SPAN + 1, block_len)[::-1]
    context = attention(qkv_rows[:, :width_local], [kv_own] + arrived, seg_ids, seg_k, slopes)
    partial = jnp.dot(context, w_out, preferred_element_type=jnp.float32).astype(jnp.bfloat16)

    partial4 = partial.reshape(n_head, rows_dev, partial.shape[1])
    sent = jnp.take(partial4, jnp.stack([head ^ 1, head ^ 3]), axis=0)
    kept = jnp.take(partial4, jnp.stack([head, head ^ 2]), axis=0)
    chip_sum = kept.astype(jnp.float32) + swapped(sent, "head", 1).astype(jnp.float32)
    other_chip = swapped(chip_sum[1].astype(jnp.bfloat16), "head", 2).astype(jnp.float32)
    hidden = (inputs + chip_sum[0] + other_chip).astype(jnp.bfloat16)
    return (hidden, key_cache, value_cache)


def solution(mesh):
    in_specs = (
        P(("seq", "head"), None),
        P(),
        P(None, None, "head"),
        P("head"),
        P("head", None),
        P("seq"),
    )
    out_specs = (P(("seq", "head"), None), P("seq", "head"), P("seq", "head"))
    return jax.shard_map(
        on_device, mesh=mesh, in_specs=in_specs, out_specs=out_specs, check_vma=False
    )
```

```python
import jax
import jax.numpy as jnp
from jax import lax
from jax.sharding import PartitionSpec as P
from jax.experimental import pallas as pl
from jax.experimental.pallas import tpu as pltpu

HD = 128
SPAN = 4


EPSILON = 1e-05
NEG_FILL = -1e30


def shifted(value, axis, steps):
    count = lax.axis_size(axis)
    leading, last = (max(0, -steps), min(count, count - steps))
    return lax.ppermute(value, axis, [(source, source + steps) for source in range(leading, last)])


def swapped(value, axis, mask):
    count = lax.axis_size(axis)
    return lax.ppermute(value, axis, [(source, source ^ mask) for source in range(count)])


def layer_norm(inputs, ln_gain):
    row_mean = jnp.mean(inputs, axis=-1, keepdims=True)
    centred = inputs - row_mean
    variance = jnp.mean(centred * centred, axis=-1, keepdims=True)
    return (centred * lax.rsqrt(variance + EPSILON) * ln_gain).astype(jnp.bfloat16)


TQ = 256
TK = 256


def attention_kernel(flags_ref, q_ref, *refs):
    span = len(refs) - 8
    kvs = refs[: span + 1]
    segq_ref, segk_ref, bias_ref, o_ref, m_sc, l_sc, acc_sc = refs[span + 1 :]
    heads = m_sc.shape[0]
    block_len = q_ref.shape[0]
    n_q = block_len // TQ
    n_t = block_len // TK
    width = heads * HD
    scale = HD ** (-0.5)
    for qt in range(n_q):
        m_sc[...] = jnp.full(m_sc.shape, NEG_FILL, jnp.float32)
        l_sc[...] = jnp.zeros(l_sc.shape, jnp.float32)
        acc_sc[...] = jnp.zeros(acc_sc.shape, jnp.float32)
        segq = segq_ref[pl.ds(qt * TQ, TQ), :]
        steps = [(0, qt)] + [(0, t) for t in range(n_t) if t * TK < qt * TQ]
        steps += [(blk, t) for blk in range(1, span + 1) for t in range(n_t)]
        for blk, t in steps:
            diag = blk == 0 and t == qt

            def body(blk=blk, t=t, diag=diag):
                segk = segk_ref[pl.ds(blk, 1), pl.ds(t * TK, TK)]
                valid = segq == segk
                if diag:
                    rows = lax.broadcasted_iota(jnp.int32, (TQ, TK), 0)
                    cols = lax.broadcasted_iota(jnp.int32, (TQ, TK), 1)
                    valid = valid & (cols <= rows)
                def one_head(h, carry):
                    lanes = pl.multiple_of(h * HD, HD)
                    q = q_ref[pl.ds(qt * TQ, TQ), pl.ds(lanes, HD)]
                    k = kvs[blk][pl.ds(t * TK, TK), pl.ds(lanes, HD)]
                    v = kvs[blk][pl.ds(t * TK, TK), pl.ds(width + lanes, HD)]
                    s = lax.dot_general(
                        q, k, (((1,), (1,)), ((), ())), preferred_element_type=jnp.float32
                    )
                    s = s * scale + bias_ref[pl.ds(h, 1), pl.ds(blk * block_len + t * TK, TK)]
                    s = jnp.where(valid, s, NEG_FILL)
                    m_prev = m_sc[h]
                    m_new = jnp.maximum(m_prev, jnp.max(s, axis=1, keepdims=True))
                    p = jnp.exp(s - m_new)
                    rescale = jnp.exp(m_prev - m_new)
                    l_sc[h] = l_sc[h] * rescale + jnp.sum(p, axis=1, keepdims=True)
                    acc_sc[h] = acc_sc[h] * rescale + jnp.dot(
                        p.astype(jnp.bfloat16), v, preferred_element_type=jnp.float32
                    )
                    m_sc[h] = m_new
                    return carry

                lax.fori_loop(0, heads, one_head, 0)

            if diag:
                body()
            else:
                pl.when(flags_ref[qt * (span + 1) * n_t + blk * n_t + t] != 0)(body)
        for h in range(heads):
            o_ref[pl.ds(qt * TQ, TQ), pl.ds(h * HD, HD)] = (acc_sc[h] / l_sc[h]).astype(o_ref.dtype)


def attention(queries, kv_blocks, seg_q, seg_k, slopes):
    block_len, width = queries.shape
    heads = width // HD
    span = len(kv_blocks) - 1
    n_q, n_t = block_len // TQ, block_len // TK
    offsets = jnp.arange(block_len, dtype=jnp.int32)
    rel = (jnp.arange(span + 1, dtype=jnp.int32)[:, None] * -block_len + offsets[None, :]).reshape(-1)
    bias = slopes[:, None] * rel.astype(jnp.float32)[None, :]
    seg_first = seg_q.reshape(n_q, TQ)[:, 0]
    seg_last = seg_k.reshape(span + 1, n_t, TK)[:, :, -1]
    flags = (seg_last[None, :, :] >= seg_first[:, None, None]).astype(jnp.int32).reshape(-1)
    seg_rows = jnp.concatenate(
        [seg_k, jnp.full(((-seg_k.shape[0]) % 8, block_len), -1, jnp.int32)], axis=0
    )
    vmem = pl.BlockSpec(memory_space=pltpu.VMEM)
    work = heads * block_len * (span + 1) * block_len
    return pl.pallas_call(
        attention_kernel,
        out_shape=jax.ShapeDtypeStruct((block_len, width), jnp.bfloat16),
        in_specs=[pl.BlockSpec(memory_space=pltpu.SMEM)] + [vmem] * (span + 5),
        out_specs=vmem,
        scratch_shapes=[
            pltpu.VMEM((heads, TQ, 1), jnp.float32),
            pltpu.VMEM((heads, TQ, 1), jnp.float32),
            pltpu.VMEM((heads, TQ, HD), jnp.float32),
        ],
        cost_estimate=pl.CostEstimate(
            flops=4 * work * HD, transcendentals=work, bytes_accessed=(span + 2) * block_len * width * 4
        ),
    )(flags, queries, *kv_blocks, seg_q.reshape(block_len, 1), seg_rows, bias)


def on_device(tokens, ln_gain, w_qkv, slopes, w_out, seg_ids):
    inputs = tokens.astype(jnp.float32)
    normed = layer_norm(inputs, ln_gain)
    rows_dev = normed.shape[0]
    head = lax.axis_index("head")
    n_head = lax.axis_size("head")

    cross = swapped(normed, "head", 2)
    partner = swapped(jnp.stack([normed, cross]), "head", 1)
    pieces = jnp.stack([normed, partner[0], cross, partner[1]])
    block_rows = jnp.concatenate(
        [lax.dynamic_index_in_dim(pieces, j ^ head, 0, keepdims=False) for j in range(n_head)], axis=0
    )

    width_local = w_qkv.shape[2]
    heads_dev = slopes.shape[0]
    joined = w_qkv.reshape(w_qkv.shape[0], 3 * width_local)
    qkv_rows = jnp.dot(block_rows, joined, preferred_element_type=jnp.float32).astype(jnp.bfloat16)
    block_len = qkv_rows.shape[0]
    key_cache = qkv_rows[:, width_local : 2 * width_local]
    value_cache = qkv_rows[:, 2 * width_local :]

    kv_own = qkv_rows[:, width_local:]
    seg_row = jnp.zeros((8, kv_own.shape[1]), jnp.bfloat16).at[0, :block_len].set(
        seg_ids.astype(jnp.bfloat16)
    )
    payload = jnp.concatenate([kv_own, seg_row], axis=0)
    arrived = [shifted(payload, "seq", steps) for steps in range(1, SPAN + 1)]

    seq_index = lax.axis_index("seq")
    present = (seq_index - jnp.arange(1, SPAN + 1, dtype=jnp.int32)) >= 0
    seg_prev = jnp.stack([got[block_len, :block_len] for got in arrived]).astype(jnp.int32)
    seg_k = jnp.concatenate([seg_ids[None, :], jnp.where(present[:, None], seg_prev, -1)], axis=0)
    context = attention(qkv_rows[:, :width_local], [payload] + arrived, seg_ids, seg_k, slopes)

    context4 = context.reshape(n_head, rows_dev, context.shape[1])

    def project(owners):
        rows = jnp.concatenate(
            [lax.dynamic_index_in_dim(context4, o, 0, keepdims=False) for o in owners], axis=0
        )
        out = jnp.dot(rows, w_out, preferred_element_type=jnp.float32).astype(jnp.bfloat16)
        return out.reshape(len(owners), rows_dev, w_out.shape[1])

    sent = project([head ^ 1, head ^ 3])
    kept = project([head, head ^ 2])
    chip_sum = kept.astype(jnp.float32) + swapped(sent, "head", 1).astype(jnp.float32)
    other_chip = swapped(chip_sum[1].astype(jnp.bfloat16), "head", 2).astype(jnp.float32)
    hidden = (inputs + chip_sum[0] + other_chip).astype(jnp.bfloat16)
    return (hidden, key_cache, value_cache)


def solution(mesh):
    in_specs = (
        P(("seq", "head"), None),
        P(),
        P(None, None, "head"),
        P("head"),
        P("head", None),
        P("seq"),
    )
    out_specs = (P(("seq", "head"), None), P("seq", "head"), P("seq", "head"))
    return jax.shard_map(
        on_device, mesh=mesh, in_specs=in_specs, out_specs=out_specs, check_vma=False
    )
```

```python
import jax
import jax.numpy as jnp
from jax import lax
from jax.sharding import PartitionSpec as P
from jax.experimental import pallas as pl
from jax.experimental.pallas import tpu as pltpu

HD = 128
SPAN = 4


EPSILON = 1e-05
NEG_FILL = -1e30


def shifted(value, axis, steps):
    count = lax.axis_size(axis)
    leading, last = (max(0, -steps), min(count, count - steps))
    return lax.ppermute(value, axis, [(source, source + steps) for source in range(leading, last)])


def swapped(value, axis, mask):
    count = lax.axis_size(axis)
    return lax.ppermute(value, axis, [(source, source ^ mask) for source in range(count)])


def layer_norm(inputs, ln_gain):
    row_mean = jnp.mean(inputs, axis=-1, keepdims=True)
    centred = inputs - row_mean
    variance = jnp.mean(centred * centred, axis=-1, keepdims=True)
    return (centred * lax.rsqrt(variance + EPSILON) * ln_gain).astype(jnp.bfloat16)


TQ = 256
TK = 256


def attention_kernel(flags_ref, q_ref, *refs):
    span = len(refs) - 8
    kvs = refs[: span + 1]
    segq_ref, segk_ref, bias_ref, o_ref, m_sc, l_sc, acc_sc = refs[span + 1 :]
    heads = m_sc.shape[0]
    block_len = q_ref.shape[0]
    n_q = block_len // TQ
    n_t = block_len // TK
    width = heads * HD
    scale = HD ** (-0.5)
    for qt in range(n_q):
        m_sc[...] = jnp.full(m_sc.shape, NEG_FILL, jnp.float32)
        l_sc[...] = jnp.zeros(l_sc.shape, jnp.float32)
        acc_sc[...] = jnp.zeros(acc_sc.shape, jnp.float32)
        segq = segq_ref[pl.ds(qt * TQ, TQ), :]
        steps = [(0, qt)] + [(0, t) for t in range(n_t) if t * TK < qt * TQ]
        steps += [(blk, t) for blk in range(1, span + 1) for t in range(n_t)]
        for blk, t in steps:
            diag = blk == 0 and t == qt

            def body(blk=blk, t=t, diag=diag):
                segk = segk_ref[pl.ds(blk, 1), pl.ds(t * TK, TK)]
                valid = segq == segk
                if diag:
                    rows = lax.broadcasted_iota(jnp.int32, (TQ, TK), 0)
                    cols = lax.broadcasted_iota(jnp.int32, (TQ, TK), 1)
                    valid = valid & (cols <= rows)
                def one_head(h, carry):
                    lanes = pl.multiple_of(h * HD, HD)
                    q = q_ref[pl.ds(qt * TQ, TQ), pl.ds(lanes, HD)]
                    k = kvs[blk][pl.ds(t * TK, TK), pl.ds(lanes, HD)]
                    v = kvs[blk][pl.ds(t * TK, TK), pl.ds(width + lanes, HD)]
                    s = lax.dot_general(
                        q, k, (((1,), (1,)), ((), ())), preferred_element_type=jnp.float32
                    )
                    s = s * scale + bias_ref[pl.ds(h, 1), pl.ds(blk * block_len + t * TK, TK)]
                    s = jnp.where(valid, s, NEG_FILL)
                    m_prev = m_sc[h]
                    m_new = jnp.maximum(m_prev, jnp.max(s, axis=1, keepdims=True))
                    p = jnp.exp(s - m_new)
                    rescale = jnp.exp(m_prev - m_new)
                    l_sc[h] = l_sc[h] * rescale + jnp.sum(p, axis=1, keepdims=True)
                    acc_sc[h] = acc_sc[h] * rescale + jnp.dot(
                        p.astype(jnp.bfloat16), v, preferred_element_type=jnp.float32
                    )
                    m_sc[h] = m_new
                    return carry

                lax.fori_loop(0, heads, one_head, 0)

            if diag:
                body()
            else:
                pl.when(flags_ref[qt * (span + 1) * n_t + blk * n_t + t] != 0)(body)
        for h in range(heads):
            o_ref[pl.ds(qt * TQ, TQ), pl.ds(h * HD, HD)] = (acc_sc[h] / l_sc[h]).astype(o_ref.dtype)


def attention(queries, kv_blocks, seg_q, seg_k, slopes):
    block_len, width = queries.shape
    heads = width // HD
    span = len(kv_blocks) - 1
    n_q, n_t = block_len // TQ, block_len // TK
    offsets = jnp.arange(block_len, dtype=jnp.int32)
    rel = (jnp.arange(span + 1, dtype=jnp.int32)[:, None] * -block_len + offsets[None, :]).reshape(-1)
    bias = slopes[:, None] * rel.astype(jnp.float32)[None, :]
    seg_first = seg_q.reshape(n_q, TQ)[:, 0]
    seg_last = seg_k.reshape(span + 1, n_t, TK)[:, :, -1]
    flags = (seg_last[None, :, :] >= seg_first[:, None, None]).astype(jnp.int32).reshape(-1)
    seg_rows = jnp.concatenate(
        [seg_k, jnp.full(((-seg_k.shape[0]) % 8, block_len), -1, jnp.int32)], axis=0
    )
    vmem = pl.BlockSpec(memory_space=pltpu.VMEM)
    work = heads * block_len * (span + 1) * block_len
    return pl.pallas_call(
        attention_kernel,
        out_shape=jax.ShapeDtypeStruct((block_len, width), jnp.bfloat16),
        in_specs=[pl.BlockSpec(memory_space=pltpu.SMEM)] + [vmem] * (span + 5),
        out_specs=vmem,
        scratch_shapes=[
            pltpu.VMEM((heads, TQ, 1), jnp.float32),
            pltpu.VMEM((heads, TQ, 1), jnp.float32),
            pltpu.VMEM((heads, TQ, HD), jnp.float32),
        ],
        cost_estimate=pl.CostEstimate(
            flops=4 * work * HD, transcendentals=work, bytes_accessed=(span + 2) * block_len * width * 4
        ),
    )(flags, queries, *kv_blocks, seg_q.reshape(block_len, 1), seg_rows, bias)


RING = 4


def moved(value, pairs):
    return lax.ppermute(value, "seq", pairs)


def relay_earlier_blocks(payload):
    count = lax.axis_size("seq")
    y = lax.axis_index("seq") % RING
    ids = range(count)
    from_z = moved(payload, [(s, s + RING) for s in ids if s + RING < count])
    from_below = moved(payload, [(s, s + 1) for s in ids if s % RING < RING - 1])
    from_wrap = moved(payload, [(s, s + RING - 1) for s in ids if s % RING == 0])
    passed_up = moved(from_below, [(s, s + 1) for s in ids if 0 < s % RING < RING - 1])
    passed_down = moved(from_z, [(s, s - 1) for s in ids if s % RING > 0])
    passed_wrap = moved(from_z, [(s, s - RING + 1) for s in ids if s % RING == RING - 1])
    passed_twice = moved(passed_down, [(s, s - 1) for s in ids if 0 < s % RING < RING - 1])
    back1 = jnp.where(y == 0, passed_wrap, from_below)
    back2 = jnp.where(y <= 1, passed_twice, passed_up)
    back3 = jnp.where(y <= 2, passed_down, from_wrap)
    return [back1, back2, back3, from_z]


def on_device(tokens, ln_gain, w_qkv, slopes, w_out, seg_ids):
    inputs = tokens.astype(jnp.float32)
    normed = layer_norm(inputs, ln_gain)
    rows_dev = normed.shape[0]
    head = lax.axis_index("head")
    n_head = lax.axis_size("head")

    cross = swapped(normed, "head", 2)
    partner = swapped(jnp.stack([normed, cross]), "head", 1)
    pieces = jnp.stack([normed, partner[0], cross, partner[1]])
    block_rows = jnp.concatenate(
        [lax.dynamic_index_in_dim(pieces, j ^ head, 0, keepdims=False) for j in range(n_head)], axis=0
    )

    width_local = w_qkv.shape[2]
    heads_dev = slopes.shape[0]
    joined = w_qkv.reshape(w_qkv.shape[0], 3 * width_local)
    qkv_rows = jnp.dot(block_rows, joined, preferred_element_type=jnp.float32).astype(jnp.bfloat16)
    block_len = qkv_rows.shape[0]
    key_cache = qkv_rows[:, width_local : 2 * width_local]
    value_cache = qkv_rows[:, 2 * width_local :]

    kv_own = qkv_rows[:, width_local:]
    seg_row = jnp.zeros((8, kv_own.shape[1]), jnp.bfloat16).at[0, :block_len].set(
        seg_ids.astype(jnp.bfloat16)
    )
    payload = jnp.concatenate([kv_own, seg_row], axis=0)
    arrived = relay_earlier_blocks(payload)

    seq_index = lax.axis_index("seq")
    present = (seq_index - jnp.arange(1, SPAN + 1, dtype=jnp.int32)) >= 0
    seg_prev = jnp.stack([got[block_len, :block_len] for got in arrived]).astype(jnp.int32)
    seg_k = jnp.concatenate([seg_ids[None, :], jnp.where(present[:, None], seg_prev, -1)], axis=0)
    context = attention(qkv_rows[:, :width_local], [payload] + arrived, seg_ids, seg_k, slopes)

    context4 = context.reshape(n_head, rows_dev, context.shape[1])

    def project(owners):
        rows = jnp.concatenate(
            [lax.dynamic_index_in_dim(context4, o, 0, keepdims=False) for o in owners], axis=0
        )
        out = jnp.dot(rows, w_out, preferred_element_type=jnp.float32).astype(jnp.bfloat16)
        return out.reshape(len(owners), rows_dev, w_out.shape[1])

    sent = project([head ^ 1, head ^ 3])
    kept = project([head, head ^ 2])
    chip_sum = kept.astype(jnp.float32) + swapped(sent, "head", 1).astype(jnp.float32)
    other_chip = swapped(chip_sum[1].astype(jnp.bfloat16), "head", 2).astype(jnp.float32)
    hidden = (inputs + chip_sum[0] + other_chip).astype(jnp.bfloat16)
    return (hidden, key_cache, value_cache)


def solution(mesh):
    in_specs = (
        P(("seq", "head"), None),
        P(),
        P(None, None, "head"),
        P("head"),
        P("head", None),
        P("seq"),
    )
    out_specs = (P(("seq", "head"), None), P("seq", "head"), P("seq", "head"))
    return jax.shard_map(
        on_device, mesh=mesh, in_specs=in_specs, out_specs=out_specs, check_vma=False
    )
```

```python
import functools

import jax
import jax.numpy as jnp
from jax import lax
from jax.sharding import PartitionSpec as P
from jax.experimental import pallas as pl
from jax.experimental.pallas import tpu as pltpu

HD = 128
SPAN = 4


EPSILON = 1e-05
NEG_FILL = -1e30


def shifted(value, axis, steps):
    count = lax.axis_size(axis)
    leading, last = (max(0, -steps), min(count, count - steps))
    return lax.ppermute(value, axis, [(source, source + steps) for source in range(leading, last)])


def swapped(value, axis, mask):
    count = lax.axis_size(axis)
    return lax.ppermute(value, axis, [(source, source ^ mask) for source in range(count)])


def layer_norm(inputs, ln_gain):
    row_mean = jnp.mean(inputs, axis=-1, keepdims=True)
    centred = inputs - row_mean
    variance = jnp.mean(centred * centred, axis=-1, keepdims=True)
    return (centred * lax.rsqrt(variance + EPSILON) * ln_gain).astype(jnp.bfloat16)


TQ = 256
TK = 256


def part_kernel(n_buf, own, flags_ref, q_ref, *refs):
    bufs = refs[:n_buf]
    (segq_ref, segk_ref, bias_ref, m_in, l_in, acc_in, m_out, l_out, acc_out, m_sc, l_sc) = refs[n_buf:]
    heads = m_sc.shape[0]
    block_len = q_ref.shape[0]
    n_q, n_t = block_len // TQ, block_len // TK
    width = heads * HD
    scale = HD ** (-0.5)
    for h in range(heads):
        m_sc[h] = m_in[:, h : h + 1]
        l_sc[h] = l_in[:, h : h + 1]
    acc_out[...] = acc_in[...]
    for qt in range(n_q):
        rows = pl.ds(qt * TQ, TQ)
        segq = segq_ref[rows, :]
        steps = [(i, t) for i in range(n_buf) for t in range(n_t)]
        if own:
            steps = [(0, qt)] + [(0, t) for t in range(n_t) if t * TK < qt * TQ] + steps[n_t:]
        for i, t in steps:
            diag = own and i == 0 and t == qt

            def body(i=i, t=t, diag=diag):
                valid = segq == segk_ref[pl.ds(i, 1), pl.ds(t * TK, TK)]
                if diag:
                    r = lax.broadcasted_iota(jnp.int32, (TQ, TK), 0)
                    c = lax.broadcasted_iota(jnp.int32, (TQ, TK), 1)
                    valid = valid & (c <= r)

                def one_head(h, carry):
                    lanes = pl.multiple_of(h * HD, HD)
                    q = q_ref[rows, pl.ds(lanes, HD)]
                    k = bufs[i][pl.ds(t * TK, TK), pl.ds(lanes, HD)]
                    v = bufs[i][pl.ds(t * TK, TK), pl.ds(width + lanes, HD)]
                    s = lax.dot_general(
                        q, k, (((1,), (1,)), ((), ())), preferred_element_type=jnp.float32
                    )
                    s = s * scale + bias_ref[pl.ds(i * heads + h, 1), pl.ds(t * TK, TK)]
                    s = jnp.where(valid, s, NEG_FILL)
                    m_prev = m_sc[h, rows, :]
                    m_new = jnp.maximum(m_prev, jnp.max(s, axis=1, keepdims=True))
                    p = jnp.exp(s - m_new)
                    rescale = jnp.exp(m_prev - m_new)
                    l_sc[h, rows, :] = l_sc[h, rows, :] * rescale + jnp.sum(p, axis=1, keepdims=True)
                    acc_out[rows, pl.ds(lanes, HD)] = acc_out[rows, pl.ds(lanes, HD)] * rescale + jnp.dot(
                        p.astype(jnp.bfloat16), v, preferred_element_type=jnp.float32
                    )
                    m_sc[h, rows, :] = m_new
                    return carry

                lax.fori_loop(0, heads, one_head, 0)

            if diag:
                body()
            else:
                pl.when(flags_ref[(qt * n_buf + i) * n_t + t] != 0)(body)
    lane = lax.broadcasted_iota(jnp.int32, m_in.shape, 1)
    m_all, l_all = m_in[...], l_in[...]
    for h in range(heads):
        m_all = jnp.where(lane == h, m_sc[h], m_all)
        l_all = jnp.where(lane == h, l_sc[h], l_all)
    m_out[...] = m_all
    l_out[...] = l_all


def attention_part(state, queries, seg_q, slopes, bufs, steps_back, present, own=False):
    block_len, width = queries.shape
    heads = width // HD
    n_buf = len(bufs)
    n_q, n_t = block_len // TQ, block_len // TK
    seg_k = jnp.stack(
        [
            jnp.where(ok, buf[block_len, :block_len].astype(jnp.int32), -1)
            for buf, ok in zip(bufs, present)
        ]
    )
    if own:
        seg_k = seg_k.at[0].set(seg_q)
    seg_first = seg_q.reshape(n_q, TQ)[:, 0]
    seg_last = seg_k.reshape(n_buf, n_t, TK)[:, :, -1]
    flags = seg_last[None, :, :] >= seg_first[:, None, None]
    if own:
        earlier = jnp.arange(n_t)[None, :] < jnp.arange(n_q)[:, None]
        flags = flags.at[:, 0, :].set(flags[:, 0, :] & earlier)
    flags = flags.astype(jnp.int32).reshape(-1)
    seg_rows = jnp.concatenate(
        [seg_k, jnp.full(((-n_buf) % 8, block_len), -1, jnp.int32)], axis=0
    )
    offsets = jnp.arange(block_len, dtype=jnp.int32)
    rel = offsets[None, :] - jnp.stack(steps_back)[:, None] * block_len
    bias = (rel.astype(jnp.float32)[:, None, :] * slopes[None, :, None]).reshape(n_buf * heads, block_len)
    bias = jnp.concatenate([bias, jnp.zeros(((-n_buf * heads) % 8, block_len), jnp.float32)], axis=0)
    vmem = pl.BlockSpec(memory_space=pltpu.VMEM)
    work = heads * block_len * n_buf * block_len
    m, l, acc = state
    return pl.pallas_call(
        functools.partial(part_kernel, n_buf, own),
        out_shape=(
            jax.ShapeDtypeStruct(m.shape, jnp.float32),
            jax.ShapeDtypeStruct(l.shape, jnp.float32),
            jax.ShapeDtypeStruct(acc.shape, jnp.float32),
        ),
        in_specs=[pl.BlockSpec(memory_space=pltpu.SMEM)] + [vmem] * (n_buf + 7),
        out_specs=(vmem, vmem, vmem),
        scratch_shapes=[
            pltpu.VMEM((heads, block_len, 1), jnp.float32),
            pltpu.VMEM((heads, block_len, 1), jnp.float32),
        ],
        cost_estimate=pl.CostEstimate(
            flops=4 * work * HD,
            transcendentals=work,
            bytes_accessed=(n_buf + 4) * block_len * width * 4,
        ),
    )(flags, queries, *bufs, seg_q.reshape(block_len, 1), seg_rows, bias, m, l, acc)

RING = 4


def moved(value, pairs):
    return lax.ppermute(value, "seq", pairs)


def relay_earlier_blocks(payload):
    count = lax.axis_size("seq")
    y = lax.axis_index("seq") % RING
    ids = range(count)
    from_z = moved(payload, [(s, s + RING) for s in ids if s + RING < count])
    from_below = moved(payload, [(s, s + 1) for s in ids if s % RING < RING - 1])
    from_wrap = moved(payload, [(s, s + RING - 1) for s in ids if s % RING == 0])
    passed_up = moved(from_below, [(s, s + 1) for s in ids if 0 < s % RING < RING - 1])
    passed_down = moved(from_z, [(s, s - 1) for s in ids if s % RING > 0])
    passed_wrap = moved(from_z, [(s, s - RING + 1) for s in ids if s % RING == RING - 1])
    passed_twice = moved(passed_down, [(s, s - 1) for s in ids if 0 < s % RING < RING - 1])
    seq_index = lax.axis_index("seq")
    rounds = [
        [(from_z, 4, seq_index >= 4), (from_below, 1, y >= 1), (from_wrap, 3, y == 3)],
        [
            (passed_up, 2, y >= 2),
            (passed_down, 3, (y <= 2) & (seq_index >= 3)),
            (passed_wrap, 1, (y == 0) & (seq_index >= 1)),
        ],
        [(passed_twice, 2, (y <= 1) & (seq_index >= 2))],
    ]
    return rounds


def on_device(tokens, ln_gain, w_qkv, slopes, w_out, seg_ids):
    inputs = tokens.astype(jnp.float32)
    normed = layer_norm(inputs, ln_gain)
    rows_dev = normed.shape[0]
    head = lax.axis_index("head")
    n_head = lax.axis_size("head")

    cross = swapped(normed, "head", 2)
    partner = swapped(jnp.stack([normed, cross]), "head", 1)
    pieces = jnp.stack([normed, partner[0], cross, partner[1]])
    block_rows = jnp.concatenate(
        [lax.dynamic_index_in_dim(pieces, j ^ head, 0, keepdims=False) for j in range(n_head)], axis=0
    )

    width_local = w_qkv.shape[2]
    heads_dev = slopes.shape[0]
    joined = w_qkv.reshape(w_qkv.shape[0], 3 * width_local)
    qkv_rows = jnp.dot(block_rows, joined, preferred_element_type=jnp.float32).astype(jnp.bfloat16)
    block_len = qkv_rows.shape[0]
    key_cache = qkv_rows[:, width_local : 2 * width_local]
    value_cache = qkv_rows[:, 2 * width_local :]

    kv_own = qkv_rows[:, width_local:]
    seg_row = jnp.zeros((8, kv_own.shape[1]), jnp.bfloat16).at[0, :block_len].set(
        seg_ids.astype(jnp.bfloat16)
    )
    payload = jnp.concatenate([kv_own, seg_row], axis=0)
    rounds = relay_earlier_blocks(payload)

    queries = qkv_rows[:, :width_local]
    state = (
        jnp.full((block_len, HD), NEG_FILL, jnp.float32),
        jnp.zeros((block_len, HD), jnp.float32),
        jnp.zeros((block_len, width_local), jnp.float32),
    )
    state = attention_part(
        state, queries, seg_ids, slopes, [payload], [jnp.int32(0)], [jnp.bool_(True)], own=True
    )
    for arrived in rounds:
        bufs, steps_back, present = zip(*arrived)
        steps_back = [jnp.int32(k) for k in steps_back]
        state = attention_part(state, queries, seg_ids, slopes, list(bufs), steps_back, list(present))
    _, total, acc = state
    denominator = jnp.repeat(total[:, :heads_dev], HD, axis=1)
    context = (acc / denominator).astype(jnp.bfloat16)

    context4 = context.reshape(n_head, rows_dev, context.shape[1])

    def project(owners):
        rows = jnp.concatenate(
            [lax.dynamic_index_in_dim(context4, o, 0, keepdims=False) for o in owners], axis=0
        )
        out = jnp.dot(rows, w_out, preferred_element_type=jnp.float32).astype(jnp.bfloat16)
        return out.reshape(len(owners), rows_dev, w_out.shape[1])

    sent = project([head ^ 1, head ^ 3])
    kept = project([head, head ^ 2])
    chip_sum = kept.astype(jnp.float32) + swapped(sent, "head", 1).astype(jnp.float32)
    other_chip = swapped(chip_sum[1].astype(jnp.bfloat16), "head", 2).astype(jnp.float32)
    hidden = (inputs + chip_sum[0] + other_chip).astype(jnp.bfloat16)
    return (hidden, key_cache, value_cache)


def solution(mesh):
    in_specs = (
        P(("seq", "head"), None),
        P(),
        P(None, None, "head"),
        P("head"),
        P("head", None),
        P("seq"),
    )
    out_specs = (P(("seq", "head"), None), P("seq", "head"), P("seq", "head"))
    return jax.shard_map(
        on_device, mesh=mesh, in_specs=in_specs, out_specs=out_specs, check_vma=False
    )
```

```python
import jax
import jax.numpy as jnp
from jax import lax
from jax.sharding import PartitionSpec as P
from jax.experimental import pallas as pl
from jax.experimental.pallas import tpu as pltpu

HD = 128
SPAN = 4


EPSILON = 1e-05
NEG_FILL = -1e30


def shifted(value, axis, steps):
    count = lax.axis_size(axis)
    leading, last = (max(0, -steps), min(count, count - steps))
    return lax.ppermute(value, axis, [(source, source + steps) for source in range(leading, last)])


def swapped(value, axis, mask):
    count = lax.axis_size(axis)
    return lax.ppermute(value, axis, [(source, source ^ mask) for source in range(count)])


def layer_norm(inputs, ln_gain):
    row_mean = jnp.mean(inputs, axis=-1, keepdims=True)
    centred = inputs - row_mean
    variance = jnp.mean(centred * centred, axis=-1, keepdims=True)
    return (centred * lax.rsqrt(variance + EPSILON) * ln_gain).astype(jnp.bfloat16)


TQ = 256
TK = 256


def attention_kernel(flags_ref, q_ref, *refs):
    span = len(refs) - 8
    kvs = refs[: span + 1]
    segq_ref, segk_ref, bias_ref, o_ref, m_sc, l_sc, acc_sc = refs[span + 1 :]
    heads = m_sc.shape[0]
    block_len = q_ref.shape[0]
    n_q = block_len // TQ
    n_t = block_len // TK
    width = heads * HD
    scale = HD ** (-0.5)
    for qt in range(n_q):
        m_sc[...] = jnp.full(m_sc.shape, NEG_FILL, jnp.float32)
        l_sc[...] = jnp.zeros(l_sc.shape, jnp.float32)
        acc_sc[...] = jnp.zeros(acc_sc.shape, jnp.float32)
        segq = segq_ref[pl.ds(qt * TQ, TQ), :]
        steps = [(0, qt)] + [(0, t) for t in range(n_t) if t * TK < qt * TQ]
        steps += [(blk, t) for blk in range(1, span + 1) for t in range(n_t)]
        for blk, t in steps:
            diag = blk == 0 and t == qt

            def body(blk=blk, t=t, diag=diag):
                segk = segk_ref[pl.ds(blk, 1), pl.ds(t * TK, TK)]
                valid = segq == segk
                if diag:
                    rows = lax.broadcasted_iota(jnp.int32, (TQ, TK), 0)
                    cols = lax.broadcasted_iota(jnp.int32, (TQ, TK), 1)
                    valid = valid & (cols <= rows)
                def one_head(h, carry):
                    lanes = pl.multiple_of(h * HD, HD)
                    q = q_ref[pl.ds(qt * TQ, TQ), pl.ds(lanes, HD)]
                    k = kvs[blk][pl.ds(t * TK, TK), pl.ds(lanes, HD)]
                    v = kvs[blk][pl.ds(t * TK, TK), pl.ds(width + lanes, HD)]
                    s = lax.dot_general(
                        q, k, (((1,), (1,)), ((), ())), preferred_element_type=jnp.float32
                    )
                    s = s * scale + bias_ref[pl.ds(h, 1), pl.ds(blk * block_len + t * TK, TK)]
                    s = jnp.where(valid, s, NEG_FILL)
                    m_prev = m_sc[h]
                    m_new = jnp.maximum(m_prev, jnp.max(s, axis=1, keepdims=True))
                    p = jnp.exp(s - m_new)
                    rescale = jnp.exp(m_prev - m_new)
                    l_sc[h] = l_sc[h] * rescale + jnp.sum(p, axis=1, keepdims=True)
                    acc_sc[h] = acc_sc[h] * rescale + jnp.dot(
                        p.astype(jnp.bfloat16), v, preferred_element_type=jnp.float32
                    )
                    m_sc[h] = m_new
                    return carry

                lax.fori_loop(0, heads, one_head, 0)

            if diag:
                body()
            else:
                pl.when(flags_ref[qt * (span + 1) * n_t + blk * n_t + t] != 0)(body)
        for h in range(heads):
            o_ref[pl.ds(qt * TQ, TQ), pl.ds(h * HD, HD)] = (acc_sc[h] / l_sc[h]).astype(o_ref.dtype)


def attention(queries, kv_blocks, seg_q, seg_k, slopes):
    block_len, width = queries.shape
    heads = width // HD
    span = len(kv_blocks) - 1
    n_q, n_t = block_len // TQ, block_len // TK
    offsets = jnp.arange(block_len, dtype=jnp.int32)
    rel = (jnp.arange(span + 1, dtype=jnp.int32)[:, None] * -block_len + offsets[None, :]).reshape(-1)
    bias = slopes[:, None] * rel.astype(jnp.float32)[None, :]
    seg_first = seg_q.reshape(n_q, TQ)[:, 0]
    seg_last = seg_k.reshape(span + 1, n_t, TK)[:, :, -1]
    flags = (seg_last[None, :, :] >= seg_first[:, None, None]).astype(jnp.int32).reshape(-1)
    seg_rows = jnp.concatenate(
        [seg_k, jnp.full(((-seg_k.shape[0]) % 8, block_len), -1, jnp.int32)], axis=0
    )
    vmem = pl.BlockSpec(memory_space=pltpu.VMEM)
    work = heads * block_len * (span + 1) * block_len
    return pl.pallas_call(
        attention_kernel,
        out_shape=jax.ShapeDtypeStruct((block_len, width), jnp.bfloat16),
        in_specs=[pl.BlockSpec(memory_space=pltpu.SMEM)] + [vmem] * (span + 5),
        out_specs=vmem,
        scratch_shapes=[
            pltpu.VMEM((heads, TQ, 1), jnp.float32),
            pltpu.VMEM((heads, TQ, 1), jnp.float32),
            pltpu.VMEM((heads, TQ, HD), jnp.float32),
        ],
        cost_estimate=pl.CostEstimate(
            flops=4 * work * HD, transcendentals=work, bytes_accessed=(span + 2) * block_len * width * 4
        ),
    )(flags, queries, *kv_blocks, seg_q.reshape(block_len, 1), seg_rows, bias)


RING = 4


def moved(value, pairs):
    return lax.ppermute(value, "seq", pairs)


def relay_earlier_blocks(payload):
    count = lax.axis_size("seq")
    y = lax.axis_index("seq") % RING
    ids = range(count)
    from_z = moved(payload, [(s, s + RING) for s in ids if s + RING < count])
    from_below = moved(payload, [(s, s + 1) for s in ids if s % RING < RING - 1])
    from_wrap = moved(payload, [(s, s + RING - 1) for s in ids if s % RING == 0])
    passed_up = moved(from_below, [(s, s + 1) for s in ids if 0 < s % RING < RING - 1])
    passed_down = moved(from_z, [(s, s - 1) for s in ids if s % RING > 0])
    passed_wrap = moved(from_z, [(s, s - RING + 1) for s in ids if s % RING == RING - 1])
    passed_twice = moved(passed_down, [(s, s - 1) for s in ids if 0 < s % RING < RING - 1])
    back1 = jnp.where(y == 0, passed_wrap, from_below)
    back2 = jnp.where(y <= 1, passed_twice, passed_up)
    back3 = jnp.where(y <= 2, passed_down, from_wrap)
    return [back1, back2, back3, from_z]


def on_device(tokens, ln_gain, w_qkv, slopes, w_out, seg_ids):
    inputs = tokens.astype(jnp.float32)
    normed = layer_norm(inputs, ln_gain)
    rows_dev = normed.shape[0]
    head = lax.axis_index("head")
    n_head = lax.axis_size("head")

    width_local = w_qkv.shape[2]
    heads_dev = slopes.shape[0]
    joined = w_qkv.reshape(w_qkv.shape[0], 3 * width_local)

    def project_rows(rows):
        return jnp.dot(rows, joined, preferred_element_type=jnp.float32).astype(jnp.bfloat16)

    from_partner = swapped(normed, "head", 1)
    from_cross = swapped(normed, "head", 2)
    from_partner_cross = swapped(from_cross, "head", 1)
    pieces = jnp.stack(
        [project_rows(r) for r in (normed, from_partner, from_cross, from_partner_cross)]
    )
    qkv_rows = jnp.concatenate(
        [lax.dynamic_index_in_dim(pieces, j ^ head, 0, keepdims=False) for j in range(n_head)], axis=0
    )
    block_len = qkv_rows.shape[0]
    key_cache = qkv_rows[:, width_local : 2 * width_local]
    value_cache = qkv_rows[:, 2 * width_local :]

    kv_own = qkv_rows[:, width_local:]
    seg_row = jnp.zeros((8, kv_own.shape[1]), jnp.bfloat16).at[0, :block_len].set(
        seg_ids.astype(jnp.bfloat16)
    )
    payload = jnp.concatenate([kv_own, seg_row], axis=0)
    arrived = relay_earlier_blocks(payload)

    seq_index = lax.axis_index("seq")
    present = (seq_index - jnp.arange(1, SPAN + 1, dtype=jnp.int32)) >= 0
    seg_prev = jnp.stack([got[block_len, :block_len] for got in arrived]).astype(jnp.int32)
    seg_k = jnp.concatenate([seg_ids[None, :], jnp.where(present[:, None], seg_prev, -1)], axis=0)
    context = attention(qkv_rows[:, :width_local], [payload] + arrived, seg_ids, seg_k, slopes)

    context4 = context.reshape(n_head, rows_dev, context.shape[1])

    def project(owners):
        rows = jnp.concatenate(
            [lax.dynamic_index_in_dim(context4, o, 0, keepdims=False) for o in owners], axis=0
        )
        out = jnp.dot(rows, w_out, preferred_element_type=jnp.float32).astype(jnp.bfloat16)
        return out.reshape(len(owners), rows_dev, w_out.shape[1])

    sent = project([head ^ 1, head ^ 3])
    kept = project([head, head ^ 2])
    chip_sum = kept.astype(jnp.float32) + swapped(sent, "head", 1).astype(jnp.float32)
    other_chip = swapped(chip_sum[1].astype(jnp.bfloat16), "head", 2).astype(jnp.float32)
    hidden = (inputs + chip_sum[0] + other_chip).astype(jnp.bfloat16)
    return (hidden, key_cache, value_cache)


def solution(mesh):
    in_specs = (
        P(("seq", "head"), None),
        P(),
        P(None, None, "head"),
        P("head"),
        P("head", None),
        P("seq"),
    )
    out_specs = (P(("seq", "head"), None), P("seq", "head"), P("seq", "head"))
    return jax.shard_map(
        on_device, mesh=mesh, in_specs=in_specs, out_specs=out_specs, check_vma=False
    )
```

```python
import functools

import jax
import jax.numpy as jnp
from jax import lax
from jax.sharding import PartitionSpec as P
from jax.experimental import pallas as pl
from jax.experimental.pallas import tpu as pltpu

HD = 128
SPAN = 4


EPSILON = 1e-05
NEG_FILL = -1e30


def shifted(value, axis, steps):
    count = lax.axis_size(axis)
    leading, last = (max(0, -steps), min(count, count - steps))
    return lax.ppermute(value, axis, [(source, source + steps) for source in range(leading, last)])


def swapped(value, axis, mask):
    count = lax.axis_size(axis)
    return lax.ppermute(value, axis, [(source, source ^ mask) for source in range(count)])


def layer_norm(inputs, ln_gain):
    row_mean = jnp.mean(inputs, axis=-1, keepdims=True)
    centred = inputs - row_mean
    variance = jnp.mean(centred * centred, axis=-1, keepdims=True)
    return (centred * lax.rsqrt(variance + EPSILON) * ln_gain).astype(jnp.bfloat16)


TQ = 256
TK = 256


def part_kernel(n_buf, own, flags_ref, q_ref, *refs):
    bufs = refs[:n_buf]
    (segq_ref, segk_ref, bias_ref, m_in, l_in, acc_in, m_out, l_out, acc_out, m_sc, l_sc) = refs[n_buf:]
    heads = m_sc.shape[0]
    block_len = q_ref.shape[0]
    n_q, n_t = block_len // TQ, block_len // TK
    width = heads * HD
    scale = HD ** (-0.5)
    for h in range(heads):
        m_sc[h] = m_in[:, h : h + 1]
        l_sc[h] = l_in[:, h : h + 1]
    acc_out[...] = acc_in[...]
    for qt in range(n_q):
        rows = pl.ds(qt * TQ, TQ)
        segq = segq_ref[rows, :]
        steps = [(i, t) for i in range(n_buf) for t in range(n_t)]
        if own:
            steps = [(0, qt)] + [(0, t) for t in range(n_t) if t * TK < qt * TQ] + steps[n_t:]
        for i, t in steps:
            diag = own and i == 0 and t == qt

            def body(i=i, t=t, diag=diag):
                valid = segq == segk_ref[pl.ds(i, 1), pl.ds(t * TK, TK)]
                if diag:
                    r = lax.broadcasted_iota(jnp.int32, (TQ, TK), 0)
                    c = lax.broadcasted_iota(jnp.int32, (TQ, TK), 1)
                    valid = valid & (c <= r)

                def one_head(h, carry):
                    lanes = pl.multiple_of(h * HD, HD)
                    q = q_ref[rows, pl.ds(lanes, HD)]
                    k = bufs[i][pl.ds(t * TK, TK), pl.ds(lanes, HD)]
                    v = bufs[i][pl.ds(t * TK, TK), pl.ds(width + lanes, HD)]
                    s = lax.dot_general(
                        q, k, (((1,), (1,)), ((), ())), preferred_element_type=jnp.float32
                    )
                    s = s * scale + bias_ref[pl.ds(i * heads + h, 1), pl.ds(t * TK, TK)]
                    s = jnp.where(valid, s, NEG_FILL)
                    m_prev = m_sc[h, rows, :]
                    m_new = jnp.maximum(m_prev, jnp.max(s, axis=1, keepdims=True))
                    p = jnp.exp(s - m_new)
                    rescale = jnp.exp(m_prev - m_new)
                    l_sc[h, rows, :] = l_sc[h, rows, :] * rescale + jnp.sum(p, axis=1, keepdims=True)
                    acc_out[rows, pl.ds(lanes, HD)] = acc_out[rows, pl.ds(lanes, HD)] * rescale + jnp.dot(
                        p.astype(jnp.bfloat16), v, preferred_element_type=jnp.float32
                    )
                    m_sc[h, rows, :] = m_new
                    return carry

                lax.fori_loop(0, heads, one_head, 0)

            if diag:
                body()
            else:
                pl.when(flags_ref[(qt * n_buf + i) * n_t + t] != 0)(body)
    lane = lax.broadcasted_iota(jnp.int32, m_in.shape, 1)
    m_all, l_all = m_in[...], l_in[...]
    for h in range(heads):
        m_all = jnp.where(lane == h, m_sc[h], m_all)
        l_all = jnp.where(lane == h, l_sc[h], l_all)
    m_out[...] = m_all
    l_out[...] = l_all


def attention_part(state, queries, seg_q, slopes, bufs, steps_back, present, own=False):
    block_len, width = queries.shape
    heads = width // HD
    n_buf = len(bufs)
    n_q, n_t = block_len // TQ, block_len // TK
    seg_k = jnp.stack(
        [
            jnp.where(ok, buf[block_len, :block_len].astype(jnp.int32), -1)
            for buf, ok in zip(bufs, present)
        ]
    )
    if own:
        seg_k = seg_k.at[0].set(seg_q)
    seg_first = seg_q.reshape(n_q, TQ)[:, 0]
    seg_last = seg_k.reshape(n_buf, n_t, TK)[:, :, -1]
    flags = seg_last[None, :, :] >= seg_first[:, None, None]
    if own:
        earlier = jnp.arange(n_t)[None, :] < jnp.arange(n_q)[:, None]
        flags = flags.at[:, 0, :].set(flags[:, 0, :] & earlier)
    flags = flags.astype(jnp.int32).reshape(-1)
    seg_rows = jnp.concatenate(
        [seg_k, jnp.full(((-n_buf) % 8, block_len), -1, jnp.int32)], axis=0
    )
    offsets = jnp.arange(block_len, dtype=jnp.int32)
    rel = offsets[None, :] - jnp.stack(steps_back)[:, None] * block_len
    bias = (rel.astype(jnp.float32)[:, None, :] * slopes[None, :, None]).reshape(n_buf * heads, block_len)
    bias = jnp.concatenate([bias, jnp.zeros(((-n_buf * heads) % 8, block_len), jnp.float32)], axis=0)
    vmem = pl.BlockSpec(memory_space=pltpu.VMEM)
    work = heads * block_len * n_buf * block_len
    m, l, acc = state
    return pl.pallas_call(
        functools.partial(part_kernel, n_buf, own),
        out_shape=(
            jax.ShapeDtypeStruct(m.shape, jnp.float32),
            jax.ShapeDtypeStruct(l.shape, jnp.float32),
            jax.ShapeDtypeStruct(acc.shape, jnp.float32),
        ),
        in_specs=[pl.BlockSpec(memory_space=pltpu.SMEM)] + [vmem] * (n_buf + 7),
        out_specs=(vmem, vmem, vmem),
        scratch_shapes=[
            pltpu.VMEM((heads, block_len, 1), jnp.float32),
            pltpu.VMEM((heads, block_len, 1), jnp.float32),
        ],
        cost_estimate=pl.CostEstimate(
            flops=4 * work * HD,
            transcendentals=work,
            bytes_accessed=(n_buf + 4) * block_len * width * 4,
        ),
    )(flags, queries, *bufs, seg_q.reshape(block_len, 1), seg_rows, bias, m, l, acc)

RING = 4


def moved(value, pairs):
    return lax.ppermute(value, "seq", pairs)


def relay_earlier_blocks(payload):
    count = lax.axis_size("seq")
    y = lax.axis_index("seq") % RING
    ids = range(count)
    from_z = moved(payload, [(s, s + RING) for s in ids if s + RING < count])
    from_below = moved(payload, [(s, s + 1) for s in ids if s % RING < RING - 1])
    from_wrap = moved(payload, [(s, s + RING - 1) for s in ids if s % RING == 0])
    passed_up = moved(from_below, [(s, s + 1) for s in ids if 0 < s % RING < RING - 1])
    passed_down = moved(from_z, [(s, s - 1) for s in ids if s % RING > 0])
    passed_wrap = moved(from_z, [(s, s - RING + 1) for s in ids if s % RING == RING - 1])
    passed_twice = moved(passed_down, [(s, s - 1) for s in ids if 0 < s % RING < RING - 1])
    back1 = jnp.where(y == 0, passed_wrap, from_below)
    back2 = jnp.where(y <= 1, passed_twice, passed_up)
    back3 = jnp.where(y <= 2, passed_down, from_wrap)
    return [back1, back2, back3, from_z]


def on_device(tokens, ln_gain, w_qkv, slopes, w_out, seg_ids):
    inputs = tokens.astype(jnp.float32)
    normed = layer_norm(inputs, ln_gain)
    rows_dev = normed.shape[0]
    head = lax.axis_index("head")
    n_head = lax.axis_size("head")

    width_local = w_qkv.shape[2]
    heads_dev = slopes.shape[0]
    joined = w_qkv.reshape(w_qkv.shape[0], 3 * width_local)

    def project_rows(rows):
        return jnp.dot(rows, joined, preferred_element_type=jnp.float32).astype(jnp.bfloat16)

    from_partner = swapped(normed, "head", 1)
    from_cross = swapped(normed, "head", 2)
    from_partner_cross = swapped(from_cross, "head", 1)
    pieces = jnp.stack(
        [project_rows(r) for r in (normed, from_partner, from_cross, from_partner_cross)]
    )
    qkv_rows = jnp.concatenate(
        [lax.dynamic_index_in_dim(pieces, j ^ head, 0, keepdims=False) for j in range(n_head)], axis=0
    )
    block_len = qkv_rows.shape[0]
    key_cache = qkv_rows[:, width_local : 2 * width_local]
    value_cache = qkv_rows[:, 2 * width_local :]

    kv_own = qkv_rows[:, width_local:]
    seg_row = jnp.zeros((8, kv_own.shape[1]), jnp.bfloat16).at[0, :block_len].set(
        seg_ids.astype(jnp.bfloat16)
    )
    payload = jnp.concatenate([kv_own, seg_row], axis=0)
    arrived = relay_earlier_blocks(payload)

    queries = qkv_rows[:, :width_local]
    state = (
        jnp.full((block_len, HD), NEG_FILL, jnp.float32),
        jnp.zeros((block_len, HD), jnp.float32),
        jnp.zeros((block_len, width_local), jnp.float32),
    )
    back1, back2, back3, from_z = arrived
    seq_index_now = lax.axis_index("seq")
    state = attention_part(
        state,
        queries,
        seg_ids,
        slopes,
        [payload, from_z, back1, back3],
        [jnp.int32(0), jnp.int32(4), jnp.int32(1), jnp.int32(3)],
        [jnp.bool_(True), seq_index_now >= 4, seq_index_now >= 1, seq_index_now >= 3],
        own=True,
    )
    state = attention_part(
        state, queries, seg_ids, slopes, [back2], [jnp.int32(2)], [seq_index_now >= 2]
    )
    _, total, acc = state
    denominator = jnp.repeat(total[:, :heads_dev], HD, axis=1)
    context = (acc / denominator).astype(jnp.bfloat16)

    context4 = context.reshape(n_head, rows_dev, context.shape[1])

    def project(owners):
        rows = jnp.concatenate(
            [lax.dynamic_index_in_dim(context4, o, 0, keepdims=False) for o in owners], axis=0
        )
        out = jnp.dot(rows, w_out, preferred_element_type=jnp.float32).astype(jnp.bfloat16)
        return out.reshape(len(owners), rows_dev, w_out.shape[1])

    sent = project([head ^ 1, head ^ 3])
    kept = project([head, head ^ 2])
    chip_sum = kept.astype(jnp.float32) + swapped(sent, "head", 1).astype(jnp.float32)
    other_chip = swapped(chip_sum[1].astype(jnp.bfloat16), "head", 2).astype(jnp.float32)
    hidden = (inputs + chip_sum[0] + other_chip).astype(jnp.bfloat16)
    return (hidden, key_cache, value_cache)


def solution(mesh):
    in_specs = (
        P(("seq", "head"), None),
        P(),
        P(None, None, "head"),
        P("head"),
        P("head", None),
        P("seq"),
    )
    out_specs = (P(("seq", "head"), None), P("seq", "head"), P("seq", "head"))
    return jax.shard_map(
        on_device, mesh=mesh, in_specs=in_specs, out_specs=out_specs, check_vma=False
    )
```

```python
import functools

import jax
import jax.numpy as jnp
from jax import lax
from jax.sharding import PartitionSpec as P
from jax.experimental import pallas as pl
from jax.experimental.pallas import tpu as pltpu

HD = 128
SPAN = 4


EPSILON = 1e-05
NEG_FILL = -1e30


def shifted(value, axis, steps):
    count = lax.axis_size(axis)
    leading, last = (max(0, -steps), min(count, count - steps))
    return lax.ppermute(value, axis, [(source, source + steps) for source in range(leading, last)])


def swapped(value, axis, mask):
    count = lax.axis_size(axis)
    return lax.ppermute(value, axis, [(source, source ^ mask) for source in range(count)])


def layer_norm(inputs, ln_gain):
    row_mean = jnp.mean(inputs, axis=-1, keepdims=True)
    centred = inputs - row_mean
    variance = jnp.mean(centred * centred, axis=-1, keepdims=True)
    return (centred * lax.rsqrt(variance + EPSILON) * ln_gain).astype(jnp.bfloat16)


TQ = 256
TK = 256


def part_kernel(n_buf, own, flags_ref, q_ref, *refs):
    bufs = refs[:n_buf]
    (segq_ref, segk_ref, bias_ref, m_in, l_in, acc_in, m_out, l_out, acc_out, m_sc, l_sc) = refs[n_buf:]
    heads = m_sc.shape[0]
    block_len = q_ref.shape[0]
    n_q, n_t = block_len // TQ, block_len // TK
    width = heads * HD
    scale = HD ** (-0.5)
    for h in range(heads):
        m_sc[h] = m_in[:, h : h + 1]
        l_sc[h] = l_in[:, h : h + 1]
    acc_out[...] = acc_in[...]
    for qt in range(n_q):
        rows = pl.ds(qt * TQ, TQ)
        segq = segq_ref[rows, :]
        steps = [(i, t) for i in range(n_buf) for t in range(n_t)]
        if own:
            steps = [(0, qt)] + [(0, t) for t in range(n_t) if t * TK < qt * TQ] + steps[n_t:]
        for i, t in steps:
            diag = own and i == 0 and t == qt

            def body(i=i, t=t, diag=diag):
                valid = segq == segk_ref[pl.ds(i, 1), pl.ds(t * TK, TK)]
                if diag:
                    r = lax.broadcasted_iota(jnp.int32, (TQ, TK), 0)
                    c = lax.broadcasted_iota(jnp.int32, (TQ, TK), 1)
                    valid = valid & (c <= r)

                def one_head(h, carry):
                    lanes = pl.multiple_of(h * HD, HD)
                    q = q_ref[rows, pl.ds(lanes, HD)]
                    k = bufs[i][pl.ds(t * TK, TK), pl.ds(lanes, HD)]
                    v = bufs[i][pl.ds(t * TK, TK), pl.ds(width + lanes, HD)]
                    s = lax.dot_general(
                        q, k, (((1,), (1,)), ((), ())), preferred_element_type=jnp.float32
                    )
                    s = s * scale + bias_ref[pl.ds(i * heads + h, 1), pl.ds(t * TK, TK)]
                    s = jnp.where(valid, s, NEG_FILL)
                    m_prev = m_sc[h, rows, :]
                    m_new = jnp.maximum(m_prev, jnp.max(s, axis=1, keepdims=True))
                    p = jnp.exp(s - m_new)
                    rescale = jnp.exp(m_prev - m_new)
                    l_sc[h, rows, :] = l_sc[h, rows, :] * rescale + jnp.sum(p, axis=1, keepdims=True)
                    acc_out[rows, pl.ds(lanes, HD)] = acc_out[rows, pl.ds(lanes, HD)] * rescale + jnp.dot(
                        p.astype(jnp.bfloat16), v, preferred_element_type=jnp.float32
                    )
                    m_sc[h, rows, :] = m_new
                    return carry

                lax.fori_loop(0, heads, one_head, 0)

            if diag:
                body()
            else:
                pl.when(flags_ref[(qt * n_buf + i) * n_t + t] != 0)(body)
    lane = lax.broadcasted_iota(jnp.int32, m_in.shape, 1)
    m_all, l_all = m_in[...], l_in[...]
    for h in range(heads):
        m_all = jnp.where(lane == h, m_sc[h], m_all)
        l_all = jnp.where(lane == h, l_sc[h], l_all)
    m_out[...] = m_all
    l_out[...] = l_all


def attention_part(state, queries, seg_q, slopes, bufs, steps_back, present, own=False):
    block_len, width = queries.shape
    heads = width // HD
    n_buf = len(bufs)
    n_q, n_t = block_len // TQ, block_len // TK
    seg_k = jnp.stack(
        [
            jnp.where(ok, buf[block_len, :block_len].astype(jnp.int32), -1)
            for buf, ok in zip(bufs, present)
        ]
    )
    if own:
        seg_k = seg_k.at[0].set(seg_q)
    seg_first = seg_q.reshape(n_q, TQ)[:, 0]
    seg_last = seg_k.reshape(n_buf, n_t, TK)[:, :, -1]
    flags = seg_last[None, :, :] >= seg_first[:, None, None]
    if own:
        earlier = jnp.arange(n_t)[None, :] < jnp.arange(n_q)[:, None]
        flags = flags.at[:, 0, :].set(flags[:, 0, :] & earlier)
    flags = flags.astype(jnp.int32).reshape(-1)
    seg_rows = jnp.concatenate(
        [seg_k, jnp.full(((-n_buf) % 8, block_len), -1, jnp.int32)], axis=0
    )
    offsets = jnp.arange(block_len, dtype=jnp.int32)
    rel = offsets[None, :] - jnp.stack(steps_back)[:, None] * block_len
    bias = (rel.astype(jnp.float32)[:, None, :] * slopes[None, :, None]).reshape(n_buf * heads, block_len)
    bias = jnp.concatenate([bias, jnp.zeros(((-n_buf * heads) % 8, block_len), jnp.float32)], axis=0)
    vmem = pl.BlockSpec(memory_space=pltpu.VMEM)
    work = heads * block_len * n_buf * block_len
    m, l, acc = state
    return pl.pallas_call(
        functools.partial(part_kernel, n_buf, own),
        out_shape=(
            jax.ShapeDtypeStruct(m.shape, jnp.float32),
            jax.ShapeDtypeStruct(l.shape, jnp.float32),
            jax.ShapeDtypeStruct(acc.shape, jnp.float32),
        ),
        in_specs=[pl.BlockSpec(memory_space=pltpu.SMEM)] + [vmem] * (n_buf + 7),
        out_specs=(vmem, vmem, vmem),
        scratch_shapes=[
            pltpu.VMEM((heads, block_len, 1), jnp.float32),
            pltpu.VMEM((heads, block_len, 1), jnp.float32),
        ],
        cost_estimate=pl.CostEstimate(
            flops=4 * work * HD,
            transcendentals=work,
            bytes_accessed=(n_buf + 4) * block_len * width * 4,
        ),
    )(flags, queries, *bufs, seg_q.reshape(block_len, 1), seg_rows, bias, m, l, acc)

RING = 4


def moved(value, pairs):
    return lax.ppermute(value, "seq", pairs)


def relay_earlier_blocks(payload):
    count = lax.axis_size("seq")
    y = lax.axis_index("seq") % RING
    ids = range(count)
    from_z = moved(payload, [(s, s + RING) for s in ids if s + RING < count])
    from_below = moved(payload, [(s, s + 1) for s in ids if s % RING < RING - 1])
    from_wrap = moved(payload, [(s, s + RING - 1) for s in ids if s % RING == 0])
    passed_up = moved(from_below, [(s, s + 1) for s in ids if 0 < s % RING < RING - 1])
    passed_down = moved(from_z, [(s, s - 1) for s in ids if s % RING > 0])
    passed_wrap = moved(from_z, [(s, s - RING + 1) for s in ids if s % RING == RING - 1])
    passed_twice = moved(passed_down, [(s, s - 1) for s in ids if 0 < s % RING < RING - 1])
    back1 = jnp.where(y == 0, passed_wrap, from_below)
    back2 = jnp.where(y <= 1, passed_twice, passed_up)
    back3 = jnp.where(y <= 2, passed_down, from_wrap)
    return [back1, back2, back3, from_z]


def on_device(tokens, ln_gain, w_qkv, slopes, w_out, seg_ids):
    inputs = tokens.astype(jnp.float32)
    normed = layer_norm(inputs, ln_gain)
    rows_dev = normed.shape[0]
    head = lax.axis_index("head")
    n_head = lax.axis_size("head")

    width_local = w_qkv.shape[2]
    heads_dev = slopes.shape[0]
    joined = w_qkv.reshape(w_qkv.shape[0], 3 * width_local)

    def project_rows(rows):
        return jnp.dot(rows, joined, preferred_element_type=jnp.float32).astype(jnp.bfloat16)

    from_partner = swapped(normed, "head", 1)
    from_cross = swapped(normed, "head", 2)
    from_partner_cross = swapped(from_cross, "head", 1)
    near = project_rows(jnp.concatenate([normed, from_partner], axis=0))
    far = project_rows(jnp.concatenate([from_cross, from_partner_cross], axis=0))
    pieces = jnp.concatenate([near, far], axis=0).reshape(n_head, rows_dev, near.shape[1])
    qkv_rows = jnp.concatenate(
        [lax.dynamic_index_in_dim(pieces, j ^ head, 0, keepdims=False) for j in range(n_head)], axis=0
    )
    block_len = qkv_rows.shape[0]
    key_cache = qkv_rows[:, width_local : 2 * width_local]
    value_cache = qkv_rows[:, 2 * width_local :]

    kv_own = qkv_rows[:, width_local:]
    seg_row = jnp.zeros((8, kv_own.shape[1]), jnp.bfloat16).at[0, :block_len].set(
        seg_ids.astype(jnp.bfloat16)
    )
    payload = jnp.concatenate([kv_own, seg_row], axis=0)
    arrived = relay_earlier_blocks(payload)

    queries = qkv_rows[:, :width_local]
    state = (
        jnp.full((block_len, HD), NEG_FILL, jnp.float32),
        jnp.zeros((block_len, HD), jnp.float32),
        jnp.zeros((block_len, width_local), jnp.float32),
    )
    back1, back2, back3, from_z = arrived
    seq_index_now = lax.axis_index("seq")
    state = attention_part(
        state,
        queries,
        seg_ids,
        slopes,
        [payload, from_z, back1, back3],
        [jnp.int32(0), jnp.int32(4), jnp.int32(1), jnp.int32(3)],
        [jnp.bool_(True), seq_index_now >= 4, seq_index_now >= 1, seq_index_now >= 3],
        own=True,
    )
    state = attention_part(
        state, queries, seg_ids, slopes, [back2], [jnp.int32(2)], [seq_index_now >= 2]
    )
    _, total, acc = state
    denominator = jnp.repeat(total[:, :heads_dev], HD, axis=1)
    context = (acc / denominator).astype(jnp.bfloat16)

    context4 = context.reshape(n_head, rows_dev, context.shape[1])

    def project(owners):
        rows = jnp.concatenate(
            [lax.dynamic_index_in_dim(context4, o, 0, keepdims=False) for o in owners], axis=0
        )
        out = jnp.dot(rows, w_out, preferred_element_type=jnp.float32).astype(jnp.bfloat16)
        return out.reshape(len(owners), rows_dev, w_out.shape[1])

    sent = project([head ^ 1, head ^ 3])
    kept = project([head, head ^ 2])
    chip_sum = kept.astype(jnp.float32) + swapped(sent, "head", 1).astype(jnp.float32)
    other_chip = swapped(chip_sum[1].astype(jnp.bfloat16), "head", 2).astype(jnp.float32)
    hidden = (inputs + chip_sum[0] + other_chip).astype(jnp.bfloat16)
    return (hidden, key_cache, value_cache)


def solution(mesh):
    in_specs = (
        P(("seq", "head"), None),
        P(),
        P(None, None, "head"),
        P("head"),
        P("head", None),
        P("seq"),
    )
    out_specs = (P(("seq", "head"), None), P("seq", "head"), P("seq", "head"))
    return jax.shard_map(
        on_device, mesh=mesh, in_specs=in_specs, out_specs=out_specs, check_vma=False
    )
```

```python
import functools

import jax
import jax.numpy as jnp
from jax import lax
from jax.sharding import PartitionSpec as P
from jax.experimental import pallas as pl
from jax.experimental.pallas import tpu as pltpu

HD = 128
SPAN = 4


EPSILON = 1e-05
NEG_FILL = -1e30


def shifted(value, axis, steps):
    count = lax.axis_size(axis)
    leading, last = (max(0, -steps), min(count, count - steps))
    return lax.ppermute(value, axis, [(source, source + steps) for source in range(leading, last)])


def swapped(value, axis, mask):
    count = lax.axis_size(axis)
    return lax.ppermute(value, axis, [(source, source ^ mask) for source in range(count)])


def layer_norm(inputs, ln_gain):
    row_mean = jnp.mean(inputs, axis=-1, keepdims=True)
    centred = inputs - row_mean
    variance = jnp.mean(centred * centred, axis=-1, keepdims=True)
    return (centred * lax.rsqrt(variance + EPSILON) * ln_gain).astype(jnp.bfloat16)


TQ = 256
TK = 256


def part_kernel(n_buf, own, flags_ref, q_ref, *refs):
    bufs = refs[:n_buf]
    (segq_ref, segk_ref, bias_ref, m_in, l_in, acc_in, m_out, l_out, acc_out, m_sc, l_sc) = refs[n_buf:]
    heads = m_sc.shape[0]
    block_len = q_ref.shape[0]
    n_q, n_t = block_len // TQ, block_len // TK
    width = heads * HD
    scale = HD ** (-0.5)
    for h in range(heads):
        m_sc[h] = m_in[:, h : h + 1]
        l_sc[h] = l_in[:, h : h + 1]
    acc_out[...] = acc_in[...]
    for qt in range(n_q):
        rows = pl.ds(qt * TQ, TQ)
        segq = segq_ref[rows, :]
        steps = [(i, t) for i in range(n_buf) for t in range(n_t)]
        if own:
            steps = [(0, qt)] + [(0, t) for t in range(n_t) if t * TK < qt * TQ] + steps[n_t:]
        for i, t in steps:
            diag = own and i == 0 and t == qt

            def body(i=i, t=t, diag=diag):
                valid = segq == segk_ref[pl.ds(i, 1), pl.ds(t * TK, TK)]
                if diag:
                    r = lax.broadcasted_iota(jnp.int32, (TQ, TK), 0)
                    c = lax.broadcasted_iota(jnp.int32, (TQ, TK), 1)
                    valid = valid & (c <= r)

                def one_head(h, carry):
                    lanes = pl.multiple_of(h * HD, HD)
                    q = q_ref[rows, pl.ds(lanes, HD)]
                    k = bufs[i][pl.ds(t * TK, TK), pl.ds(lanes, HD)]
                    v = bufs[i][pl.ds(t * TK, TK), pl.ds(width + lanes, HD)]
                    s = lax.dot_general(
                        q, k, (((1,), (1,)), ((), ())), preferred_element_type=jnp.float32
                    )
                    s = s * scale + bias_ref[pl.ds(i * heads + h, 1), pl.ds(t * TK, TK)]
                    s = jnp.where(valid, s, NEG_FILL)
                    m_prev = m_sc[h, rows, :]
                    m_new = jnp.maximum(m_prev, jnp.max(s, axis=1, keepdims=True))
                    p = jnp.exp(s - m_new)
                    rescale = jnp.exp(m_prev - m_new)
                    l_sc[h, rows, :] = l_sc[h, rows, :] * rescale + jnp.sum(p, axis=1, keepdims=True)
                    acc_out[rows, pl.ds(lanes, HD)] = acc_out[rows, pl.ds(lanes, HD)] * rescale + jnp.dot(
                        p.astype(jnp.bfloat16), v, preferred_element_type=jnp.float32
                    )
                    m_sc[h, rows, :] = m_new
                    return carry

                lax.fori_loop(0, heads, one_head, 0)

            if diag:
                body()
            else:
                pl.when(flags_ref[(qt * n_buf + i) * n_t + t] != 0)(body)
    lane = lax.broadcasted_iota(jnp.int32, m_in.shape, 1)
    m_all, l_all = m_in[...], l_in[...]
    for h in range(heads):
        m_all = jnp.where(lane == h, m_sc[h], m_all)
        l_all = jnp.where(lane == h, l_sc[h], l_all)
    m_out[...] = m_all
    l_out[...] = l_all


def attention_part(state, queries, seg_q, slopes, bufs, steps_back, present, own=False):
    block_len, width = queries.shape
    heads = width // HD
    n_buf = len(bufs)
    n_q, n_t = block_len // TQ, block_len // TK
    seg_k = jnp.stack(
        [
            jnp.where(ok, buf[block_len, :block_len].astype(jnp.int32), -1)
            for buf, ok in zip(bufs, present)
        ]
    )
    if own:
        seg_k = seg_k.at[0].set(seg_q)
    seg_first = seg_q.reshape(n_q, TQ)[:, 0]
    seg_last = seg_k.reshape(n_buf, n_t, TK)[:, :, -1]
    flags = seg_last[None, :, :] >= seg_first[:, None, None]
    if own:
        earlier = jnp.arange(n_t)[None, :] < jnp.arange(n_q)[:, None]
        flags = flags.at[:, 0, :].set(flags[:, 0, :] & earlier)
    flags = flags.astype(jnp.int32).reshape(-1)
    seg_rows = jnp.concatenate(
        [seg_k, jnp.full(((-n_buf) % 8, block_len), -1, jnp.int32)], axis=0
    )
    offsets = jnp.arange(block_len, dtype=jnp.int32)
    rel = offsets[None, :] - jnp.stack(steps_back)[:, None] * block_len
    bias = (rel.astype(jnp.float32)[:, None, :] * slopes[None, :, None]).reshape(n_buf * heads, block_len)
    bias = jnp.concatenate([bias, jnp.zeros(((-n_buf * heads) % 8, block_len), jnp.float32)], axis=0)
    vmem = pl.BlockSpec(memory_space=pltpu.VMEM)
    work = heads * block_len * n_buf * block_len
    m, l, acc = state
    return pl.pallas_call(
        functools.partial(part_kernel, n_buf, own),
        out_shape=(
            jax.ShapeDtypeStruct(m.shape, jnp.float32),
            jax.ShapeDtypeStruct(l.shape, jnp.float32),
            jax.ShapeDtypeStruct(acc.shape, jnp.float32),
        ),
        in_specs=[pl.BlockSpec(memory_space=pltpu.SMEM)] + [vmem] * (n_buf + 7),
        out_specs=(vmem, vmem, vmem),
        scratch_shapes=[
            pltpu.VMEM((heads, block_len, 1), jnp.float32),
            pltpu.VMEM((heads, block_len, 1), jnp.float32),
        ],
        cost_estimate=pl.CostEstimate(
            flops=4 * work * HD,
            transcendentals=work,
            bytes_accessed=(n_buf + 4) * block_len * width * 4,
        ),
    )(flags, queries, *bufs, seg_q.reshape(block_len, 1), seg_rows, bias, m, l, acc)

RING = 4


def moved(value, pairs):
    return lax.ppermute(value, "seq", pairs)


def relay_earlier_blocks(payload):
    count = lax.axis_size("seq")
    y = lax.axis_index("seq") % RING
    ids = range(count)
    from_z = moved(payload, [(s, s + RING) for s in ids if s + RING < count])
    from_below = moved(payload, [(s, s + 1) for s in ids if s % RING < RING - 1])
    from_wrap = moved(payload, [(s, s + RING - 1) for s in ids if s % RING == 0])
    passed_up = moved(from_below, [(s, s + 1) for s in ids if 0 < s % RING < RING - 1])
    passed_down = moved(from_z, [(s, s - 1) for s in ids if s % RING > 0])
    passed_wrap = moved(from_z, [(s, s - RING + 1) for s in ids if s % RING == RING - 1])
    passed_twice = moved(passed_down, [(s, s - 1) for s in ids if 0 < s % RING < RING - 1])
    back1 = jnp.where(y == 0, passed_wrap, from_below)
    back2 = jnp.where(y <= 1, passed_twice, passed_up)
    back3 = jnp.where(y <= 2, passed_down, from_wrap)
    return [back1, back2, back3, from_z]


def on_device(tokens, ln_gain, w_qkv, slopes, w_out, seg_ids):
    inputs = tokens.astype(jnp.float32)
    normed = layer_norm(inputs, ln_gain)
    rows_dev = normed.shape[0]
    head = lax.axis_index("head")
    n_head = lax.axis_size("head")

    width_local = w_qkv.shape[2]
    heads_dev = slopes.shape[0]

    def project_rows(rows):
        out = jnp.einsum("rd,dtc->rtc", rows, w_qkv, preferred_element_type=jnp.float32)
        return out.astype(jnp.bfloat16).reshape(rows.shape[0], 3 * width_local)

    from_partner = swapped(normed, "head", 1)
    from_cross = swapped(normed, "head", 2)
    near = project_rows(jnp.concatenate([normed, from_partner], axis=0))
    near, from_cross = lax.optimization_barrier((near, from_cross))
    from_partner_cross = swapped(from_cross, "head", 1)
    far = project_rows(jnp.concatenate([from_cross, from_partner_cross], axis=0))
    pieces = jnp.concatenate([near, far], axis=0).reshape(n_head, rows_dev, near.shape[1])
    qkv_rows = jnp.concatenate(
        [lax.dynamic_index_in_dim(pieces, j ^ head, 0, keepdims=False) for j in range(n_head)], axis=0
    )
    block_len = qkv_rows.shape[0]
    key_cache = qkv_rows[:, width_local : 2 * width_local]
    value_cache = qkv_rows[:, 2 * width_local :]

    kv_own = qkv_rows[:, width_local:]
    seg_row = jnp.zeros((8, kv_own.shape[1]), jnp.bfloat16).at[0, :block_len].set(
        seg_ids.astype(jnp.bfloat16)
    )
    payload = jnp.concatenate([kv_own, seg_row], axis=0)
    arrived = relay_earlier_blocks(payload)

    queries = qkv_rows[:, :width_local]
    state = (
        jnp.full((block_len, HD), NEG_FILL, jnp.float32),
        jnp.zeros((block_len, HD), jnp.float32),
        jnp.zeros((block_len, width_local), jnp.float32),
    )
    back1, back2, back3, from_z = arrived
    seq_index_now = lax.axis_index("seq")
    state = attention_part(
        state,
        queries,
        seg_ids,
        slopes,
        [payload, from_z, back1, back3],
        [jnp.int32(0), jnp.int32(4), jnp.int32(1), jnp.int32(3)],
        [jnp.bool_(True), seq_index_now >= 4, seq_index_now >= 1, seq_index_now >= 3],
        own=True,
    )
    state = attention_part(
        state, queries, seg_ids, slopes, [back2], [jnp.int32(2)], [seq_index_now >= 2]
    )
    _, total, acc = state
    denominator = jnp.repeat(total[:, :heads_dev], HD, axis=1)
    context = (acc / denominator).astype(jnp.bfloat16)

    context4 = context.reshape(n_head, rows_dev, context.shape[1])

    def project(owners):
        rows = jnp.concatenate(
            [lax.dynamic_index_in_dim(context4, o, 0, keepdims=False) for o in owners], axis=0
        )
        out = jnp.dot(rows, w_out, preferred_element_type=jnp.float32).astype(jnp.bfloat16)
        return out.reshape(len(owners), rows_dev, w_out.shape[1])

    sent = project([head ^ 1, head ^ 3])
    kept = project([head, head ^ 2])
    chip_sum = kept.astype(jnp.float32) + swapped(sent, "head", 1).astype(jnp.float32)
    other_chip = swapped(chip_sum[1].astype(jnp.bfloat16), "head", 2).astype(jnp.float32)
    hidden = (inputs + chip_sum[0] + other_chip).astype(jnp.bfloat16)
    return (hidden, key_cache, value_cache)


def solution(mesh):
    in_specs = (
        P(("seq", "head"), None),
        P(),
        P(None, None, "head"),
        P("head"),
        P("head", None),
        P("seq"),
    )
    out_specs = (P(("seq", "head"), None), P("seq", "head"), P("seq", "head"))
    return jax.shard_map(
        on_device, mesh=mesh, in_specs=in_specs, out_specs=out_specs, check_vma=False
    )
```

```python
import functools

import jax
import jax.numpy as jnp
from jax import lax
from jax.sharding import PartitionSpec as P
from jax.experimental import pallas as pl
from jax.experimental.pallas import tpu as pltpu

HD = 128
SPAN = 4


EPSILON = 1e-05
NEG_FILL = -1e30


def shifted(value, axis, steps):
    count = lax.axis_size(axis)
    leading, last = (max(0, -steps), min(count, count - steps))
    return lax.ppermute(value, axis, [(source, source + steps) for source in range(leading, last)])


def swapped(value, axis, mask):
    count = lax.axis_size(axis)
    return lax.ppermute(value, axis, [(source, source ^ mask) for source in range(count)])


def layer_norm(inputs, ln_gain):
    row_mean = jnp.mean(inputs, axis=-1, keepdims=True)
    centred = inputs - row_mean
    variance = jnp.mean(centred * centred, axis=-1, keepdims=True)
    return (centred * lax.rsqrt(variance + EPSILON) * ln_gain).astype(jnp.bfloat16)


TQ = 256
TK = 256


def part_kernel(n_buf, own, flags_ref, q_ref, *refs):
    bufs = refs[:n_buf]
    (segq_ref, segk_ref, bias_ref, m_in, l_in, acc_in, m_out, l_out, acc_out, m_sc, l_sc) = refs[n_buf:]
    heads = m_sc.shape[0]
    block_len = q_ref.shape[0]
    n_q, n_t = block_len // TQ, block_len // TK
    width = heads * HD
    scale = HD ** (-0.5)
    for h in range(heads):
        m_sc[h] = m_in[:, h : h + 1]
        l_sc[h] = l_in[:, h : h + 1]
    acc_out[...] = acc_in[...]
    for qt in range(n_q):
        rows = pl.ds(qt * TQ, TQ)
        segq = segq_ref[rows, :]
        steps = [(i, t) for i in range(n_buf) for t in range(n_t)]
        if own:
            steps = [(0, qt)] + [(0, t) for t in range(n_t) if t * TK < qt * TQ] + steps[n_t:]
        for i, t in steps:
            diag = own and i == 0 and t == qt

            def body(i=i, t=t, diag=diag):
                valid = segq == segk_ref[pl.ds(i, 1), pl.ds(t * TK, TK)]
                if diag:
                    r = lax.broadcasted_iota(jnp.int32, (TQ, TK), 0)
                    c = lax.broadcasted_iota(jnp.int32, (TQ, TK), 1)
                    valid = valid & (c <= r)

                def one_head(h, carry):
                    lanes = pl.multiple_of(h * HD, HD)
                    q = q_ref[rows, pl.ds(lanes, HD)]
                    k = bufs[i][pl.ds(t * TK, TK), pl.ds(lanes, HD)]
                    v = bufs[i][pl.ds(t * TK, TK), pl.ds(width + lanes, HD)]
                    s = lax.dot_general(
                        q, k, (((1,), (1,)), ((), ())), preferred_element_type=jnp.float32
                    )
                    s = s * scale + bias_ref[pl.ds(i * heads + h, 1), pl.ds(t * TK, TK)]
                    s = jnp.where(valid, s, NEG_FILL)
                    m_prev = m_sc[h, rows, :]
                    m_new = jnp.maximum(m_prev, jnp.max(s, axis=1, keepdims=True))
                    p = jnp.exp(s - m_new)
                    rescale = jnp.exp(m_prev - m_new)
                    l_sc[h, rows, :] = l_sc[h, rows, :] * rescale + jnp.sum(p, axis=1, keepdims=True)
                    acc_out[rows, pl.ds(lanes, HD)] = acc_out[rows, pl.ds(lanes, HD)] * rescale + jnp.dot(
                        p.astype(jnp.bfloat16), v, preferred_element_type=jnp.float32
                    )
                    m_sc[h, rows, :] = m_new
                    return carry

                lax.fori_loop(0, heads, one_head, 0)

            if diag:
                body()
            else:
                pl.when(flags_ref[(qt * n_buf + i) * n_t + t] != 0)(body)
    lane = lax.broadcasted_iota(jnp.int32, m_in.shape, 1)
    m_all, l_all = m_in[...], l_in[...]
    for h in range(heads):
        m_all = jnp.where(lane == h, m_sc[h], m_all)
        l_all = jnp.where(lane == h, l_sc[h], l_all)
    m_out[...] = m_all
    l_out[...] = l_all


def attention_part(state, queries, seg_q, slopes, bufs, steps_back, present, own=False):
    block_len, width = queries.shape
    heads = width // HD
    n_buf = len(bufs)
    n_q, n_t = block_len // TQ, block_len // TK
    seg_k = jnp.stack(
        [
            jnp.where(ok, buf[block_len, :block_len].astype(jnp.int32), -1)
            for buf, ok in zip(bufs, present)
        ]
    )
    if own:
        seg_k = seg_k.at[0].set(seg_q)
    seg_first = seg_q.reshape(n_q, TQ)[:, 0]
    seg_last = seg_k.reshape(n_buf, n_t, TK)[:, :, -1]
    flags = seg_last[None, :, :] >= seg_first[:, None, None]
    if own:
        earlier = jnp.arange(n_t)[None, :] < jnp.arange(n_q)[:, None]
        flags = flags.at[:, 0, :].set(flags[:, 0, :] & earlier)
    flags = flags.astype(jnp.int32).reshape(-1)
    seg_rows = jnp.concatenate(
        [seg_k, jnp.full(((-n_buf) % 8, block_len), -1, jnp.int32)], axis=0
    )
    offsets = jnp.arange(block_len, dtype=jnp.int32)
    rel = offsets[None, :] - jnp.stack(steps_back)[:, None] * block_len
    bias = (rel.astype(jnp.float32)[:, None, :] * slopes[None, :, None]).reshape(n_buf * heads, block_len)
    bias = jnp.concatenate([bias, jnp.zeros(((-n_buf * heads) % 8, block_len), jnp.float32)], axis=0)
    vmem = pl.BlockSpec(memory_space=pltpu.VMEM)
    work = heads * block_len * n_buf * block_len
    m, l, acc = state
    return pl.pallas_call(
        functools.partial(part_kernel, n_buf, own),
        out_shape=(
            jax.ShapeDtypeStruct(m.shape, jnp.float32),
            jax.ShapeDtypeStruct(l.shape, jnp.float32),
            jax.ShapeDtypeStruct(acc.shape, jnp.float32),
        ),
        in_specs=[pl.BlockSpec(memory_space=pltpu.SMEM)] + [vmem] * (n_buf + 7),
        out_specs=(vmem, vmem, vmem),
        scratch_shapes=[
            pltpu.VMEM((heads, block_len, 1), jnp.float32),
            pltpu.VMEM((heads, block_len, 1), jnp.float32),
        ],
        cost_estimate=pl.CostEstimate(
            flops=4 * work * HD,
            transcendentals=work,
            bytes_accessed=(n_buf + 4) * block_len * width * 4,
        ),
    )(flags, queries, *bufs, seg_q.reshape(block_len, 1), seg_rows, bias, m, l, acc)

RING = 4


def moved(value, pairs):
    return lax.ppermute(value, "seq", pairs)


def relay_earlier_blocks(payload):
    count = lax.axis_size("seq")
    y = lax.axis_index("seq") % RING
    ids = range(count)
    from_z = moved(payload, [(s, s + RING) for s in ids if s + RING < count])
    from_below = moved(payload, [(s, s + 1) for s in ids if s % RING < RING - 1])
    from_wrap = moved(payload, [(s, s + RING - 1) for s in ids if s % RING == 0])
    passed_up = moved(from_below, [(s, s + 1) for s in ids if 0 < s % RING < RING - 1])
    passed_down = moved(from_z, [(s, s - 1) for s in ids if s % RING > 0])
    passed_wrap = moved(from_z, [(s, s - RING + 1) for s in ids if s % RING == RING - 1])
    passed_twice = moved(passed_down, [(s, s - 1) for s in ids if 0 < s % RING < RING - 1])
    back1 = jnp.where(y == 0, passed_wrap, from_below)
    back2 = jnp.where(y <= 1, passed_twice, passed_up)
    back3 = jnp.where(y <= 2, passed_down, from_wrap)
    return [back1, back2, back3, from_z]


def on_device(tokens, ln_gain, w_qkv, slopes, w_out, seg_ids):
    inputs = tokens.astype(jnp.float32)
    normed = layer_norm(inputs, ln_gain)
    rows_dev = normed.shape[0]
    head = lax.axis_index("head")
    n_head = lax.axis_size("head")

    width_local = w_qkv.shape[2]
    heads_dev = slopes.shape[0]
    joined = w_qkv.reshape(w_qkv.shape[0], 3 * width_local)

    def project_rows(rows):
        return jnp.dot(rows, joined, preferred_element_type=jnp.float32).astype(jnp.bfloat16)

    from_partner = swapped(normed, "head", 1)
    from_cross = swapped(normed, "head", 2)
    near = project_rows(jnp.concatenate([normed, from_partner], axis=0))
    near, from_cross = lax.optimization_barrier((near, from_cross))
    from_partner_cross = swapped(from_cross, "head", 1)
    far = project_rows(jnp.concatenate([from_cross, from_partner_cross], axis=0))
    pieces = jnp.concatenate([near, far], axis=0).reshape(n_head, rows_dev, near.shape[1])
    qkv_rows = jnp.concatenate(
        [lax.dynamic_index_in_dim(pieces, j ^ head, 0, keepdims=False) for j in range(n_head)], axis=0
    )
    block_len = qkv_rows.shape[0]
    key_cache = qkv_rows[:, width_local : 2 * width_local]
    value_cache = qkv_rows[:, 2 * width_local :]

    kv_own = qkv_rows[:, width_local:]
    seg_row = jnp.zeros((8, kv_own.shape[1]), jnp.bfloat16).at[0, :block_len].set(
        seg_ids.astype(jnp.bfloat16)
    )
    payload = jnp.concatenate([kv_own, seg_row], axis=0)
    arrived = relay_earlier_blocks(payload)

    queries = qkv_rows[:, :width_local]
    state = (
        jnp.full((block_len, HD), NEG_FILL, jnp.float32),
        jnp.zeros((block_len, HD), jnp.float32),
        jnp.zeros((block_len, width_local), jnp.float32),
    )
    back1, back2, back3, from_z = arrived
    seq_index_now = lax.axis_index("seq")
    state = attention_part(
        state,
        queries,
        seg_ids,
        slopes,
        [payload, from_z, back1, back3],
        [jnp.int32(0), jnp.int32(4), jnp.int32(1), jnp.int32(3)],
        [jnp.bool_(True), seq_index_now >= 4, seq_index_now >= 1, seq_index_now >= 3],
        own=True,
    )
    state = attention_part(
        state, queries, seg_ids, slopes, [back2], [jnp.int32(2)], [seq_index_now >= 2]
    )
    _, total, acc = state
    denominator = jnp.repeat(total[:, :heads_dev], HD, axis=1)
    context = (acc / denominator).astype(jnp.bfloat16)

    context4 = context.reshape(n_head, rows_dev, context.shape[1])

    def project(owners):
        rows = jnp.concatenate(
            [lax.dynamic_index_in_dim(context4, o, 0, keepdims=False) for o in owners], axis=0
        )
        out = jnp.dot(rows, w_out, preferred_element_type=jnp.float32).astype(jnp.bfloat16)
        return out.reshape(len(owners), rows_dev, w_out.shape[1])

    sent = project([head ^ 1, head ^ 3])
    kept = project([head, head ^ 2])
    chip_sum = kept.astype(jnp.float32) + swapped(sent, "head", 1).astype(jnp.float32)
    other_chip = swapped(chip_sum[1].astype(jnp.bfloat16), "head", 2).astype(jnp.float32)
    hidden = (inputs + chip_sum[0] + other_chip).astype(jnp.bfloat16)
    return (hidden, key_cache, value_cache)


def solution(mesh):
    in_specs = (
        P(("seq", "head"), None),
        P(),
        P(None, None, "head"),
        P("head"),
        P("head", None),
        P("seq"),
    )
    out_specs = (P(("seq", "head"), None), P("seq", "head"), P("seq", "head"))
    return jax.shard_map(
        on_device, mesh=mesh, in_specs=in_specs, out_specs=out_specs, check_vma=False
    )
```

```python
import functools

import jax
import jax.numpy as jnp
from jax import lax
from jax.sharding import PartitionSpec as P
from jax.experimental import pallas as pl
from jax.experimental.pallas import tpu as pltpu

HD = 128
SPAN = 4


EPSILON = 1e-05
NEG_FILL = -1e30


def shifted(value, axis, steps):
    count = lax.axis_size(axis)
    leading, last = (max(0, -steps), min(count, count - steps))
    return lax.ppermute(value, axis, [(source, source + steps) for source in range(leading, last)])


def swapped(value, axis, mask):
    count = lax.axis_size(axis)
    return lax.ppermute(value, axis, [(source, source ^ mask) for source in range(count)])


def layer_norm(inputs, ln_gain):
    row_mean = jnp.mean(inputs, axis=-1, keepdims=True)
    centred = inputs - row_mean
    variance = jnp.mean(centred * centred, axis=-1, keepdims=True)
    return (centred * lax.rsqrt(variance + EPSILON) * ln_gain).astype(jnp.bfloat16)


TQ = 256
TK = 256


def part_kernel(n_buf, own, flags_ref, q_ref, *refs):
    bufs = refs[:n_buf]
    (segq_ref, segk_ref, bias_ref, m_in, l_in, acc_in, m_out, l_out, acc_out, m_sc, l_sc) = refs[n_buf:]
    heads = m_sc.shape[0]
    block_len = q_ref.shape[0]
    n_q, n_t = block_len // TQ, block_len // TK
    width = heads * HD
    scale = HD ** (-0.5)
    for h in range(heads):
        m_sc[h] = m_in[:, h : h + 1]
        l_sc[h] = l_in[:, h : h + 1]
    acc_out[...] = acc_in[...]
    for qt in range(n_q):
        rows = pl.ds(qt * TQ, TQ)
        segq = segq_ref[rows, :]
        steps = [(i, t) for i in range(n_buf) for t in range(n_t)]
        if own:
            steps = [(0, qt)] + [(0, t) for t in range(n_t) if t * TK < qt * TQ] + steps[n_t:]
        for i, t in steps:
            diag = own and i == 0 and t == qt

            def body(i=i, t=t, diag=diag):
                valid = segq == segk_ref[pl.ds(i, 1), pl.ds(t * TK, TK)]
                if diag:
                    r = lax.broadcasted_iota(jnp.int32, (TQ, TK), 0)
                    c = lax.broadcasted_iota(jnp.int32, (TQ, TK), 1)
                    valid = valid & (c <= r)

                def one_head(h, carry):
                    lanes = pl.multiple_of(h * HD, HD)
                    q = q_ref[rows, pl.ds(lanes, HD)]
                    k_t = bufs[i][pl.ds(lanes, HD), pl.ds(t * TK, TK)]
                    v = bufs[i][pl.ds(t * TK, TK), pl.ds(width + lanes, HD)]
                    s = jnp.dot(q, k_t, preferred_element_type=jnp.float32)
                    s = s * scale + bias_ref[pl.ds(i * heads + h, 1), pl.ds(t * TK, TK)]
                    s = jnp.where(valid, s, NEG_FILL)
                    m_prev = m_sc[h, rows, :]
                    m_new = jnp.maximum(m_prev, jnp.max(s, axis=1, keepdims=True))
                    p = jnp.exp(s - m_new)
                    rescale = jnp.exp(m_prev - m_new)
                    l_sc[h, rows, :] = l_sc[h, rows, :] * rescale + jnp.sum(p, axis=1, keepdims=True)
                    acc_out[rows, pl.ds(lanes, HD)] = acc_out[rows, pl.ds(lanes, HD)] * rescale + jnp.dot(
                        p.astype(jnp.bfloat16), v, preferred_element_type=jnp.float32
                    )
                    m_sc[h, rows, :] = m_new
                    return carry

                lax.fori_loop(0, heads, one_head, 0)

            if diag:
                body()
            else:
                pl.when(flags_ref[(qt * n_buf + i) * n_t + t] != 0)(body)
    lane = lax.broadcasted_iota(jnp.int32, m_in.shape, 1)
    m_all, l_all = m_in[...], l_in[...]
    for h in range(heads):
        m_all = jnp.where(lane == h, m_sc[h], m_all)
        l_all = jnp.where(lane == h, l_sc[h], l_all)
    m_out[...] = m_all
    l_out[...] = l_all


def attention_part(state, queries, seg_q, slopes, bufs, steps_back, present, own=False):
    block_len, width = queries.shape
    heads = width // HD
    n_buf = len(bufs)
    n_q, n_t = block_len // TQ, block_len // TK
    seg_k = jnp.stack(
        [
            jnp.where(ok, buf[block_len, :block_len].astype(jnp.int32), -1)
            for buf, ok in zip(bufs, present)
        ]
    )
    if own:
        seg_k = seg_k.at[0].set(seg_q)
    seg_first = seg_q.reshape(n_q, TQ)[:, 0]
    seg_last = seg_k.reshape(n_buf, n_t, TK)[:, :, -1]
    flags = seg_last[None, :, :] >= seg_first[:, None, None]
    if own:
        earlier = jnp.arange(n_t)[None, :] < jnp.arange(n_q)[:, None]
        flags = flags.at[:, 0, :].set(flags[:, 0, :] & earlier)
    flags = flags.astype(jnp.int32).reshape(-1)
    seg_rows = jnp.concatenate(
        [seg_k, jnp.full(((-n_buf) % 8, block_len), -1, jnp.int32)], axis=0
    )
    offsets = jnp.arange(block_len, dtype=jnp.int32)
    rel = offsets[None, :] - jnp.stack(steps_back)[:, None] * block_len
    bias = (rel.astype(jnp.float32)[:, None, :] * slopes[None, :, None]).reshape(n_buf * heads, block_len)
    bias = jnp.concatenate([bias, jnp.zeros(((-n_buf * heads) % 8, block_len), jnp.float32)], axis=0)
    vmem = pl.BlockSpec(memory_space=pltpu.VMEM)
    work = heads * block_len * n_buf * block_len
    m, l, acc = state
    return pl.pallas_call(
        functools.partial(part_kernel, n_buf, own),
        out_shape=(
            jax.ShapeDtypeStruct(m.shape, jnp.float32),
            jax.ShapeDtypeStruct(l.shape, jnp.float32),
            jax.ShapeDtypeStruct(acc.shape, jnp.float32),
        ),
        in_specs=[pl.BlockSpec(memory_space=pltpu.SMEM)] + [vmem] * (n_buf + 7),
        out_specs=(vmem, vmem, vmem),
        scratch_shapes=[
            pltpu.VMEM((heads, block_len, 1), jnp.float32),
            pltpu.VMEM((heads, block_len, 1), jnp.float32),
        ],
        cost_estimate=pl.CostEstimate(
            flops=4 * work * HD,
            transcendentals=work,
            bytes_accessed=(n_buf + 4) * block_len * width * 4,
        ),
    )(flags, queries, *bufs, seg_q.reshape(block_len, 1), seg_rows, bias, m, l, acc)

RING = 4


def moved(value, pairs):
    return lax.ppermute(value, "seq", pairs)


def relay_earlier_blocks(payload):
    count = lax.axis_size("seq")
    y = lax.axis_index("seq") % RING
    ids = range(count)
    from_z = moved(payload, [(s, s + RING) for s in ids if s + RING < count])
    from_below = moved(payload, [(s, s + 1) for s in ids if s % RING < RING - 1])
    from_wrap = moved(payload, [(s, s + RING - 1) for s in ids if s % RING == 0])
    passed_up = moved(from_below, [(s, s + 1) for s in ids if 0 < s % RING < RING - 1])
    passed_down = moved(from_z, [(s, s - 1) for s in ids if s % RING > 0])
    passed_wrap = moved(from_z, [(s, s - RING + 1) for s in ids if s % RING == RING - 1])
    passed_twice = moved(passed_down, [(s, s - 1) for s in ids if 0 < s % RING < RING - 1])
    back1 = jnp.where(y == 0, passed_wrap, from_below)
    back2 = jnp.where(y <= 1, passed_twice, passed_up)
    back3 = jnp.where(y <= 2, passed_down, from_wrap)
    return [back1, back2, back3, from_z]


def on_device(tokens, ln_gain, w_qkv, slopes, w_out, seg_ids):
    inputs = tokens.astype(jnp.float32)
    normed = layer_norm(inputs, ln_gain)
    rows_dev = normed.shape[0]
    head = lax.axis_index("head")
    n_head = lax.axis_size("head")

    width_local = w_qkv.shape[2]
    heads_dev = slopes.shape[0]
    joined = w_qkv.reshape(w_qkv.shape[0], 3 * width_local)

    def project_rows(rows):
        return jnp.dot(rows, joined, preferred_element_type=jnp.float32).astype(jnp.bfloat16)

    from_partner = swapped(normed, "head", 1)
    from_cross = swapped(normed, "head", 2)
    near = project_rows(jnp.concatenate([normed, from_partner], axis=0))
    near, from_cross = lax.optimization_barrier((near, from_cross))
    from_partner_cross = swapped(from_cross, "head", 1)
    far = project_rows(jnp.concatenate([from_cross, from_partner_cross], axis=0))
    pieces = jnp.concatenate([near, far], axis=0).reshape(n_head, rows_dev, near.shape[1])
    qkv_rows = jnp.concatenate(
        [lax.dynamic_index_in_dim(pieces, j ^ head, 0, keepdims=False) for j in range(n_head)], axis=0
    )
    block_len = qkv_rows.shape[0]
    key_cache = qkv_rows[:, width_local : 2 * width_local]
    value_cache = qkv_rows[:, 2 * width_local :]

    kv_own = jnp.concatenate([key_cache.T, value_cache], axis=1)
    seg_row = jnp.zeros((8, kv_own.shape[1]), jnp.bfloat16).at[0, :block_len].set(
        seg_ids.astype(jnp.bfloat16)
    )
    payload = jnp.concatenate([kv_own, seg_row], axis=0)
    arrived = relay_earlier_blocks(payload)

    queries = qkv_rows[:, :width_local]
    state = (
        jnp.full((block_len, HD), NEG_FILL, jnp.float32),
        jnp.zeros((block_len, HD), jnp.float32),
        jnp.zeros((block_len, width_local), jnp.float32),
    )
    back1, back2, back3, from_z = arrived
    seq_index_now = lax.axis_index("seq")
    state = attention_part(
        state,
        queries,
        seg_ids,
        slopes,
        [payload, from_z, back1, back3],
        [jnp.int32(0), jnp.int32(4), jnp.int32(1), jnp.int32(3)],
        [jnp.bool_(True), seq_index_now >= 4, seq_index_now >= 1, seq_index_now >= 3],
        own=True,
    )
    state = attention_part(
        state, queries, seg_ids, slopes, [back2], [jnp.int32(2)], [seq_index_now >= 2]
    )
    _, total, acc = state
    denominator = jnp.repeat(total[:, :heads_dev], HD, axis=1)
    context = (acc / denominator).astype(jnp.bfloat16)

    context4 = context.reshape(n_head, rows_dev, context.shape[1])

    def project(owners):
        rows = jnp.concatenate(
            [lax.dynamic_index_in_dim(context4, o, 0, keepdims=False) for o in owners], axis=0
        )
        out = jnp.dot(rows, w_out, preferred_element_type=jnp.float32).astype(jnp.bfloat16)
        return out.reshape(len(owners), rows_dev, w_out.shape[1])

    sent = project([head ^ 1, head ^ 3])
    kept = project([head, head ^ 2])
    chip_sum = kept.astype(jnp.float32) + swapped(sent, "head", 1).astype(jnp.float32)
    other_chip = swapped(chip_sum[1].astype(jnp.bfloat16), "head", 2).astype(jnp.float32)
    hidden = (inputs + chip_sum[0] + other_chip).astype(jnp.bfloat16)
    return (hidden, key_cache, value_cache)


def solution(mesh):
    in_specs = (
        P(("seq", "head"), None),
        P(),
        P(None, None, "head"),
        P("head"),
        P("head", None),
        P("seq"),
    )
    out_specs = (P(("seq", "head"), None), P("seq", "head"), P("seq", "head"))
    return jax.shard_map(
        on_device, mesh=mesh, in_specs=in_specs, out_specs=out_specs, check_vma=False
    )
```

```python
import functools

import jax
import jax.numpy as jnp
from jax import lax
from jax.sharding import PartitionSpec as P
from jax.experimental import pallas as pl
from jax.experimental.pallas import tpu as pltpu

HD = 128
SPAN = 4


EPSILON = 1e-05
NEG_FILL = -1e30


def shifted(value, axis, steps):
    count = lax.axis_size(axis)
    leading, last = (max(0, -steps), min(count, count - steps))
    return lax.ppermute(value, axis, [(source, source + steps) for source in range(leading, last)])


def swapped(value, axis, mask):
    count = lax.axis_size(axis)
    return lax.ppermute(value, axis, [(source, source ^ mask) for source in range(count)])


def layer_norm(inputs, ln_gain):
    row_mean = jnp.mean(inputs, axis=-1, keepdims=True)
    centred = inputs - row_mean
    variance = jnp.mean(centred * centred, axis=-1, keepdims=True)
    return (centred * lax.rsqrt(variance + EPSILON) * ln_gain).astype(jnp.bfloat16)


TQ = 256
TK = 256


def part_kernel(n_buf, own, flags_ref, q_ref, *refs):
    bufs = refs[:n_buf]
    (segq_ref, segk_ref, bias_ref, m_in, l_in, acc_in, m_out, l_out, acc_out, m_sc, l_sc) = refs[n_buf:]
    heads = m_sc.shape[0]
    block_len = q_ref.shape[0]
    n_q, n_t = block_len // TQ, block_len // TK
    width = heads * HD
    scale = HD ** (-0.5)
    for h in range(heads):
        m_sc[h] = m_in[:, h : h + 1]
        l_sc[h] = l_in[:, h : h + 1]
    acc_out[...] = acc_in[...]
    for qt in range(n_q):
        rows = pl.ds(qt * TQ, TQ)
        segq = segq_ref[rows, :]
        steps = [(i, t) for i in range(n_buf) for t in range(n_t)]
        if own:
            steps = [(0, qt)] + [(0, t) for t in range(n_t) if t * TK < qt * TQ] + steps[n_t:]
        for i, t in steps:
            diag = own and i == 0 and t == qt

            def body(i=i, t=t, diag=diag):
                valid = segq == segk_ref[pl.ds(i, 1), pl.ds(t * TK, TK)]
                if diag:
                    r = lax.broadcasted_iota(jnp.int32, (TQ, TK), 0)
                    c = lax.broadcasted_iota(jnp.int32, (TQ, TK), 1)
                    valid = valid & (c <= r)

                def one_head(h, carry):
                    lanes = pl.multiple_of(h * HD, HD)
                    q = q_ref[rows, pl.ds(lanes, HD)]
                    k_t = bufs[i][pl.ds(lanes, HD), pl.ds(t * TK, TK)]
                    v = bufs[i][pl.ds(t * TK, TK), pl.ds(width + lanes, HD)]
                    s = jnp.dot(q, k_t, preferred_element_type=jnp.float32)
                    s = s * scale + bias_ref[pl.ds(i * heads + h, 1), pl.ds(t * TK, TK)]
                    s = jnp.where(valid, s, NEG_FILL)
                    m_prev = m_sc[h, rows, :]
                    m_new = jnp.maximum(m_prev, jnp.max(s, axis=1, keepdims=True))
                    p = jnp.exp(s - m_new)
                    rescale = jnp.exp(m_prev - m_new)
                    l_sc[h, rows, :] = l_sc[h, rows, :] * rescale + jnp.sum(p, axis=1, keepdims=True)
                    acc_out[rows, pl.ds(lanes, HD)] = acc_out[rows, pl.ds(lanes, HD)] * rescale + jnp.dot(
                        p.astype(jnp.bfloat16), v, preferred_element_type=jnp.float32
                    )
                    m_sc[h, rows, :] = m_new
                    return carry

                lax.fori_loop(0, heads, one_head, 0)

            if diag:
                body()
            else:
                pl.when(flags_ref[(qt * n_buf + i) * n_t + t] != 0)(body)
    lane = lax.broadcasted_iota(jnp.int32, m_in.shape, 1)
    m_all, l_all = m_in[...], l_in[...]
    for h in range(heads):
        m_all = jnp.where(lane == h, m_sc[h], m_all)
        l_all = jnp.where(lane == h, l_sc[h], l_all)
    m_out[...] = m_all
    l_out[...] = l_all


def attention_part(state, queries, seg_q, slopes, bufs, steps_back, present, own=False):
    block_len, width = queries.shape
    heads = width // HD
    n_buf = len(bufs)
    n_q, n_t = block_len // TQ, block_len // TK
    seg_k = jnp.stack(
        [
            jnp.where(ok, buf[block_len, :block_len].astype(jnp.int32), -1)
            for buf, ok in zip(bufs, present)
        ]
    )
    if own:
        seg_k = seg_k.at[0].set(seg_q)
    seg_first = seg_q.reshape(n_q, TQ)[:, 0]
    seg_last = seg_k.reshape(n_buf, n_t, TK)[:, :, -1]
    flags = seg_last[None, :, :] >= seg_first[:, None, None]
    if own:
        earlier = jnp.arange(n_t)[None, :] < jnp.arange(n_q)[:, None]
        flags = flags.at[:, 0, :].set(flags[:, 0, :] & earlier)
    flags = flags.astype(jnp.int32).reshape(-1)
    seg_rows = jnp.concatenate(
        [seg_k, jnp.full(((-n_buf) % 8, block_len), -1, jnp.int32)], axis=0
    )
    offsets = jnp.arange(block_len, dtype=jnp.int32)
    rel = offsets[None, :] - jnp.stack(steps_back)[:, None] * block_len
    bias = (rel.astype(jnp.float32)[:, None, :] * slopes[None, :, None]).reshape(n_buf * heads, block_len)
    bias = jnp.concatenate([bias, jnp.zeros(((-n_buf * heads) % 8, block_len), jnp.float32)], axis=0)
    vmem = pl.BlockSpec(memory_space=pltpu.VMEM)
    work = heads * block_len * n_buf * block_len
    m, l, acc = state
    return pl.pallas_call(
        functools.partial(part_kernel, n_buf, own),
        out_shape=(
            jax.ShapeDtypeStruct(m.shape, jnp.float32),
            jax.ShapeDtypeStruct(l.shape, jnp.float32),
            jax.ShapeDtypeStruct(acc.shape, jnp.float32),
        ),
        in_specs=[pl.BlockSpec(memory_space=pltpu.SMEM)] + [vmem] * (n_buf + 7),
        out_specs=(vmem, vmem, vmem),
        scratch_shapes=[
            pltpu.VMEM((heads, block_len, 1), jnp.float32),
            pltpu.VMEM((heads, block_len, 1), jnp.float32),
        ],
        cost_estimate=pl.CostEstimate(
            flops=4 * work * HD,
            transcendentals=work,
            bytes_accessed=(n_buf + 4) * block_len * width * 4,
        ),
    )(flags, queries, *bufs, seg_q.reshape(block_len, 1), seg_rows, bias, m, l, acc)

RING = 4


def moved(value, pairs):
    return lax.ppermute(value, "seq", pairs)


def relay_earlier_blocks(payload):
    count = lax.axis_size("seq")
    y = lax.axis_index("seq") % RING
    ids = range(count)
    from_z = moved(payload, [(s, s + RING) for s in ids if s + RING < count])
    from_below = moved(payload, [(s, s + 1) for s in ids if s % RING < RING - 1])
    from_wrap = moved(payload, [(s, s + RING - 1) for s in ids if s % RING == 0])
    passed_up = moved(from_below, [(s, s + 1) for s in ids if 0 < s % RING < RING - 1])
    passed_down = moved(from_z, [(s, s - 1) for s in ids if s % RING > 0])
    passed_wrap = moved(from_z, [(s, s - RING + 1) for s in ids if s % RING == RING - 1])
    passed_twice = moved(passed_down, [(s, s - 1) for s in ids if 0 < s % RING < RING - 1])
    back1 = jnp.where(y == 0, passed_wrap, from_below)
    back2 = jnp.where(y <= 1, passed_twice, passed_up)
    back3 = jnp.where(y <= 2, passed_down, from_wrap)
    return [back1, back2, back3, from_z]


def on_device(tokens, ln_gain, w_qkv, slopes, w_out, seg_ids):
    inputs = tokens.astype(jnp.float32)
    normed = layer_norm(inputs, ln_gain)
    rows_dev = normed.shape[0]
    head = lax.axis_index("head")
    n_head = lax.axis_size("head")

    width_local = w_qkv.shape[2]
    heads_dev = slopes.shape[0]
    joined = w_qkv.reshape(w_qkv.shape[0], 3 * width_local)

    def project_rows(rows):
        return jnp.dot(rows, joined, preferred_element_type=jnp.float32).astype(jnp.bfloat16)

    from_partner = swapped(normed, "head", 1)
    from_cross = swapped(normed, "head", 2)
    from_partner_cross = swapped(from_cross, "head", 1)
    near = project_rows(jnp.concatenate([normed, from_partner], axis=0))
    far = project_rows(jnp.concatenate([from_cross, from_partner_cross], axis=0))
    pieces = jnp.concatenate([near, far], axis=0).reshape(n_head, rows_dev, near.shape[1])
    qkv_rows = jnp.concatenate(
        [lax.dynamic_index_in_dim(pieces, j ^ head, 0, keepdims=False) for j in range(n_head)], axis=0
    )
    block_len = qkv_rows.shape[0]
    key_cache = qkv_rows[:, width_local : 2 * width_local]
    value_cache = qkv_rows[:, 2 * width_local :]

    kv_own = jnp.concatenate([key_cache.T, value_cache], axis=1)
    seg_row = jnp.zeros((8, kv_own.shape[1]), jnp.bfloat16).at[0, :block_len].set(
        seg_ids.astype(jnp.bfloat16)
    )
    payload = jnp.concatenate([kv_own, seg_row], axis=0)
    arrived = relay_earlier_blocks(payload)

    queries = qkv_rows[:, :width_local]
    state = (
        jnp.full((block_len, HD), NEG_FILL, jnp.float32),
        jnp.zeros((block_len, HD), jnp.float32),
        jnp.zeros((block_len, width_local), jnp.float32),
    )
    back1, back2, back3, from_z = arrived
    seq_index_now = lax.axis_index("seq")
    state = attention_part(
        state,
        queries,
        seg_ids,
        slopes,
        [payload, from_z, back1, back3],
        [jnp.int32(0), jnp.int32(4), jnp.int32(1), jnp.int32(3)],
        [jnp.bool_(True), seq_index_now >= 4, seq_index_now >= 1, seq_index_now >= 3],
        own=True,
    )
    state = attention_part(
        state, queries, seg_ids, slopes, [back2], [jnp.int32(2)], [seq_index_now >= 2]
    )
    _, total, acc = state
    denominator = jnp.repeat(total[:, :heads_dev], HD, axis=1)
    context = (acc / denominator).astype(jnp.bfloat16)

    context4 = context.reshape(n_head, rows_dev, context.shape[1])

    def project(owners):
        rows = jnp.concatenate(
            [lax.dynamic_index_in_dim(context4, o, 0, keepdims=False) for o in owners], axis=0
        )
        out = jnp.dot(rows, w_out, preferred_element_type=jnp.float32).astype(jnp.bfloat16)
        return out.reshape(len(owners), rows_dev, w_out.shape[1])

    sent = project([head ^ 1, head ^ 3])
    kept = project([head, head ^ 2])
    chip_sum = kept.astype(jnp.float32) + swapped(sent, "head", 1).astype(jnp.float32)
    other_chip = swapped(chip_sum[1].astype(jnp.bfloat16), "head", 2).astype(jnp.float32)
    hidden = (inputs + chip_sum[0] + other_chip).astype(jnp.bfloat16)
    return (hidden, key_cache, value_cache)


def solution(mesh):
    in_specs = (
        P(("seq", "head"), None),
        P(),
        P(None, None, "head"),
        P("head"),
        P("head", None),
        P("seq"),
    )
    out_specs = (P(("seq", "head"), None), P("seq", "head"), P("seq", "head"))
    return jax.shard_map(
        on_device, mesh=mesh, in_specs=in_specs, out_specs=out_specs, check_vma=False
    )
```

```python
import functools

import jax
import jax.numpy as jnp
from jax import lax
from jax.sharding import PartitionSpec as P
from jax.experimental import pallas as pl
from jax.experimental.pallas import tpu as pltpu

HD = 128
SPAN = 4


EPSILON = 1e-05
NEG_FILL = -1e30


def shifted(value, axis, steps):
    count = lax.axis_size(axis)
    leading, last = (max(0, -steps), min(count, count - steps))
    return lax.ppermute(value, axis, [(source, source + steps) for source in range(leading, last)])


def swapped(value, axis, mask):
    count = lax.axis_size(axis)
    return lax.ppermute(value, axis, [(source, source ^ mask) for source in range(count)])


def layer_norm(inputs, ln_gain):
    row_mean = jnp.mean(inputs, axis=-1, keepdims=True)
    centred = inputs - row_mean
    variance = jnp.mean(centred * centred, axis=-1, keepdims=True)
    return (centred * lax.rsqrt(variance + EPSILON) * ln_gain).astype(jnp.bfloat16)


TQ = 256
TK = 256


def part_kernel(n_buf, own, last, flags_ref, q_ref, *refs):
    bufs = refs[:n_buf]
    segq_ref, segk_ref, bias_ref = refs[n_buf : n_buf + 3]
    rest = list(refs[n_buf + 3 :])
    if not own:
        m_in, l_in, acc_in = rest[:3]
        rest = rest[3:]
    if last:
        ctx_ref = rest.pop(0)
    else:
        m_out, l_out, acc_out = rest[:3]
        rest = rest[3:]
    m_sc, l_sc, acc_sc = rest
    heads = m_sc.shape[0]
    block_len = q_ref.shape[0]
    n_q, n_t = block_len // TQ, block_len // TK
    width = heads * HD
    scale = HD ** (-0.5)
    if own:
        m_sc[...] = jnp.full(m_sc.shape, NEG_FILL, jnp.float32)
        l_sc[...] = jnp.zeros(l_sc.shape, jnp.float32)
        acc_sc[...] = jnp.zeros(acc_sc.shape, jnp.float32)
    else:
        for h in range(heads):
            m_sc[h] = m_in[:, h : h + 1]
            l_sc[h] = l_in[:, h : h + 1]
        acc_sc[...] = acc_in[...]
    for qt in range(n_q):
        rows = pl.ds(qt * TQ, TQ)
        segq = segq_ref[rows, :]
        steps = [(i, t) for i in range(n_buf) for t in range(n_t)]
        if own:
            steps = [(0, qt)] + [(0, t) for t in range(n_t) if t * TK < qt * TQ] + steps[n_t:]
        for i, t in steps:
            diag = own and i == 0 and t == qt

            def body(i=i, t=t, diag=diag):
                valid = segq == segk_ref[pl.ds(i, 1), pl.ds(t * TK, TK)]
                if diag:
                    r = lax.broadcasted_iota(jnp.int32, (TQ, TK), 0)
                    c = lax.broadcasted_iota(jnp.int32, (TQ, TK), 1)
                    valid = valid & (c <= r)

                def one_head(h, carry):
                    lanes = pl.multiple_of(h * HD, HD)
                    q = q_ref[rows, pl.ds(lanes, HD)]
                    k_t = bufs[i][pl.ds(lanes, HD), pl.ds(t * TK, TK)]
                    v = bufs[i][pl.ds(t * TK, TK), pl.ds(width + lanes, HD)]
                    s = jnp.dot(q, k_t, preferred_element_type=jnp.float32)
                    s = s * scale + bias_ref[pl.ds(i * heads + h, 1), pl.ds(t * TK, TK)]
                    s = jnp.where(valid, s, NEG_FILL)
                    m_prev = m_sc[h, rows, :]
                    m_new = jnp.maximum(m_prev, jnp.max(s, axis=1, keepdims=True))
                    p = jnp.exp(s - m_new)
                    rescale = jnp.exp(m_prev - m_new)
                    l_sc[h, rows, :] = l_sc[h, rows, :] * rescale + jnp.sum(p, axis=1, keepdims=True)
                    acc_sc[rows, pl.ds(lanes, HD)] = acc_sc[rows, pl.ds(lanes, HD)] * rescale + jnp.dot(
                        p.astype(jnp.bfloat16), v, preferred_element_type=jnp.float32
                    )
                    m_sc[h, rows, :] = m_new
                    return carry

                lax.fori_loop(0, heads, one_head, 0)

            if diag:
                body()
            else:
                pl.when(flags_ref[(qt * n_buf + i) * n_t + t] != 0)(body)
    if last:
        for h in range(heads):
            cols = pl.ds(h * HD, HD)
            ctx_ref[:, cols] = (acc_sc[:, cols] / l_sc[h]).astype(ctx_ref.dtype)
        return
    lane = lax.broadcasted_iota(jnp.int32, m_out.shape, 1)
    m_all = jnp.zeros(m_out.shape, jnp.float32)
    l_all = jnp.zeros(l_out.shape, jnp.float32)
    for h in range(heads):
        m_all = jnp.where(lane == h, m_sc[h], m_all)
        l_all = jnp.where(lane == h, l_sc[h], l_all)
    m_out[...] = m_all
    l_out[...] = l_all
    acc_out[...] = acc_sc[...]


def attention_part(state, queries, seg_q, slopes, bufs, steps_back, present, own=False, last=False):
    block_len, width = queries.shape
    heads = width // HD
    n_buf = len(bufs)
    n_q, n_t = block_len // TQ, block_len // TK
    seg_k = jnp.stack(
        [
            jnp.where(ok, buf[block_len, :block_len].astype(jnp.int32), -1)
            for buf, ok in zip(bufs, present)
        ]
    )
    if own:
        seg_k = seg_k.at[0].set(seg_q)
    seg_first = seg_q.reshape(n_q, TQ)[:, 0]
    seg_last = seg_k.reshape(n_buf, n_t, TK)[:, :, -1]
    flags = seg_last[None, :, :] >= seg_first[:, None, None]
    if own:
        earlier = jnp.arange(n_t)[None, :] < jnp.arange(n_q)[:, None]
        flags = flags.at[:, 0, :].set(flags[:, 0, :] & earlier)
    flags = flags.astype(jnp.int32).reshape(-1)
    seg_rows = jnp.concatenate(
        [seg_k, jnp.full(((-n_buf) % 8, block_len), -1, jnp.int32)], axis=0
    )
    offsets = jnp.arange(block_len, dtype=jnp.int32)
    rel = offsets[None, :] - jnp.stack(steps_back)[:, None] * block_len
    bias = (rel.astype(jnp.float32)[:, None, :] * slopes[None, :, None]).reshape(n_buf * heads, block_len)
    bias = jnp.concatenate([bias, jnp.zeros(((-n_buf * heads) % 8, block_len), jnp.float32)], axis=0)
    vmem = pl.BlockSpec(memory_space=pltpu.VMEM)
    work = heads * block_len * n_buf * block_len
    state = () if own else tuple(state)
    if last:
        out_shape = jax.ShapeDtypeStruct((block_len, width), jnp.bfloat16)
        out_specs = vmem
    else:
        out_shape = (
            jax.ShapeDtypeStruct((block_len, HD), jnp.float32),
            jax.ShapeDtypeStruct((block_len, HD), jnp.float32),
            jax.ShapeDtypeStruct((block_len, width), jnp.float32),
        )
        out_specs = (vmem, vmem, vmem)
    return pl.pallas_call(
        functools.partial(part_kernel, n_buf, own, last),
        out_shape=out_shape,
        in_specs=[pl.BlockSpec(memory_space=pltpu.SMEM)] + [vmem] * (n_buf + 4 + len(state)),
        out_specs=out_specs,
        scratch_shapes=[
            pltpu.VMEM((heads, block_len, 1), jnp.float32),
            pltpu.VMEM((heads, block_len, 1), jnp.float32),
            pltpu.VMEM((block_len, width), jnp.float32),
        ],
        cost_estimate=pl.CostEstimate(
            flops=4 * work * HD,
            transcendentals=work,
            bytes_accessed=(n_buf + 4) * block_len * width * 4,
        ),
    )(flags, queries, *bufs, seg_q.reshape(block_len, 1), seg_rows, bias, *state)

RING = 4


def moved(value, pairs):
    return lax.ppermute(value, "seq", pairs)


def relay_earlier_blocks(payload):
    count = lax.axis_size("seq")
    y = lax.axis_index("seq") % RING
    ids = range(count)
    from_z = moved(payload, [(s, s + RING) for s in ids if s + RING < count])
    from_below = moved(payload, [(s, s + 1) for s in ids if s % RING < RING - 1])
    from_wrap = moved(payload, [(s, s + RING - 1) for s in ids if s % RING == 0])
    passed_up = moved(from_below, [(s, s + 1) for s in ids if 0 < s % RING < RING - 1])
    passed_down = moved(from_z, [(s, s - 1) for s in ids if s % RING > 0])
    passed_wrap = moved(from_z, [(s, s - RING + 1) for s in ids if s % RING == RING - 1])
    passed_twice = moved(passed_down, [(s, s - 1) for s in ids if 0 < s % RING < RING - 1])
    back1 = jnp.where(y == 0, passed_wrap, from_below)
    back2 = jnp.where(y <= 1, passed_twice, passed_up)
    back3 = jnp.where(y <= 2, passed_down, from_wrap)
    return [back1, back2, back3, from_z]


def on_device(tokens, ln_gain, w_qkv, slopes, w_out, seg_ids):
    inputs = tokens.astype(jnp.float32)
    normed = layer_norm(inputs, ln_gain)
    rows_dev = normed.shape[0]
    head = lax.axis_index("head")
    n_head = lax.axis_size("head")

    width_local = w_qkv.shape[2]
    heads_dev = slopes.shape[0]
    joined = w_qkv.reshape(w_qkv.shape[0], 3 * width_local)

    def project_rows(rows):
        return jnp.dot(rows, joined, preferred_element_type=jnp.float32).astype(jnp.bfloat16)

    from_partner = swapped(normed, "head", 1)
    from_cross = swapped(normed, "head", 2)
    from_partner_cross = swapped(from_cross, "head", 1)
    near = project_rows(jnp.concatenate([normed, from_partner], axis=0))
    far = project_rows(jnp.concatenate([from_cross, from_partner_cross], axis=0))
    pieces = jnp.concatenate([near, far], axis=0).reshape(n_head, rows_dev, near.shape[1])
    qkv_rows = jnp.concatenate(
        [lax.dynamic_index_in_dim(pieces, j ^ head, 0, keepdims=False) for j in range(n_head)], axis=0
    )
    block_len = qkv_rows.shape[0]
    key_cache = qkv_rows[:, width_local : 2 * width_local]
    value_cache = qkv_rows[:, 2 * width_local :]

    kv_own = jnp.concatenate([key_cache.T, value_cache], axis=1)
    seg_row = jnp.zeros((8, kv_own.shape[1]), jnp.bfloat16).at[0, :block_len].set(
        seg_ids.astype(jnp.bfloat16)
    )
    payload = jnp.concatenate([kv_own, seg_row], axis=0)
    arrived = relay_earlier_blocks(payload)

    queries = qkv_rows[:, :width_local]
    back1, back2, back3, from_z = arrived
    seq_index_now = lax.axis_index("seq")
    state = attention_part(
        None,
        queries,
        seg_ids,
        slopes,
        [payload, from_z, back1, back3],
        [jnp.int32(0), jnp.int32(4), jnp.int32(1), jnp.int32(3)],
        [jnp.bool_(True), seq_index_now >= 4, seq_index_now >= 1, seq_index_now >= 3],
        own=True,
    )
    context = attention_part(
        state, queries, seg_ids, slopes, [back2], [jnp.int32(2)], [seq_index_now >= 2], last=True
    )

    context4 = context.reshape(n_head, rows_dev, context.shape[1])

    def project(owners):
        rows = jnp.concatenate(
            [lax.dynamic_index_in_dim(context4, o, 0, keepdims=False) for o in owners], axis=0
        )
        out = jnp.dot(rows, w_out, preferred_element_type=jnp.float32).astype(jnp.bfloat16)
        return out.reshape(len(owners), rows_dev, w_out.shape[1])

    sent = project([head ^ 1, head ^ 3])
    kept = project([head, head ^ 2])
    chip_sum = kept.astype(jnp.float32) + swapped(sent, "head", 1).astype(jnp.float32)
    other_chip = swapped(chip_sum[1].astype(jnp.bfloat16), "head", 2).astype(jnp.float32)
    hidden = (inputs + chip_sum[0] + other_chip).astype(jnp.bfloat16)
    return (hidden, key_cache, value_cache)


def solution(mesh):
    in_specs = (
        P(("seq", "head"), None),
        P(),
        P(None, None, "head"),
        P("head"),
        P("head", None),
        P("seq"),
    )
    out_specs = (P(("seq", "head"), None), P("seq", "head"), P("seq", "head"))
    return jax.shard_map(
        on_device, mesh=mesh, in_specs=in_specs, out_specs=out_specs, check_vma=False
    )
```

```python
import functools

import jax
import jax.numpy as jnp
from jax import lax
from jax.sharding import PartitionSpec as P
from jax.experimental import pallas as pl
from jax.experimental.pallas import tpu as pltpu

HD = 128
SPAN = 4


EPSILON = 1e-05
NEG_FILL = -1e30


def shifted(value, axis, steps):
    count = lax.axis_size(axis)
    leading, last = (max(0, -steps), min(count, count - steps))
    return lax.ppermute(value, axis, [(source, source + steps) for source in range(leading, last)])


def swapped(value, axis, mask):
    count = lax.axis_size(axis)
    return lax.ppermute(value, axis, [(source, source ^ mask) for source in range(count)])


def layer_norm(inputs, ln_gain):
    row_mean = jnp.mean(inputs, axis=-1, keepdims=True)
    centred = inputs - row_mean
    variance = jnp.mean(centred * centred, axis=-1, keepdims=True)
    return (centred * lax.rsqrt(variance + EPSILON) * ln_gain).astype(jnp.bfloat16)


TQ = 256
TK = 256


def part_kernel(n_buf, own, last, flags_ref, q_ref, *refs):
    bufs = refs[:n_buf]
    segq_ref, segk_ref, bias_ref = refs[n_buf : n_buf + 3]
    rest = list(refs[n_buf + 3 :])
    if not own:
        m_in, l_in, acc_in = rest[:3]
        rest = rest[3:]
    if last:
        ctx_ref = rest.pop(0)
    else:
        m_out, l_out, acc_out = rest[:3]
        rest = rest[3:]
    m_sc, l_sc, acc_sc = rest
    heads = m_sc.shape[0]
    block_len = q_ref.shape[0]
    n_q, n_t = block_len // TQ, block_len // TK
    width = heads * HD
    scale = HD ** (-0.5)
    if own:
        m_sc[...] = jnp.full(m_sc.shape, NEG_FILL, jnp.float32)
        l_sc[...] = jnp.zeros(l_sc.shape, jnp.float32)
        acc_sc[...] = jnp.zeros(acc_sc.shape, jnp.float32)
    else:
        for h in range(heads):
            m_sc[h] = m_in[:, h : h + 1]
            l_sc[h] = l_in[:, h : h + 1]
        acc_sc[...] = acc_in[...]
    for qt in range(n_q):
        rows = pl.ds(qt * TQ, TQ)
        segq = segq_ref[rows, :]
        steps = [(i, t) for i in range(n_buf) for t in range(n_t)]
        if own:
            steps = [(0, qt)] + [(0, t) for t in range(n_t) if t * TK < qt * TQ] + steps[n_t:]
        for i, t in steps:
            diag = own and i == 0 and t == qt

            def body(i=i, t=t, diag=diag):
                valid = segq == segk_ref[pl.ds(i, 1), pl.ds(t * TK, TK)]
                if diag:
                    r = lax.broadcasted_iota(jnp.int32, (TQ, TK), 0)
                    c = lax.broadcasted_iota(jnp.int32, (TQ, TK), 1)
                    valid = valid & (c <= r)

                def one_head(h, carry):
                    lanes = pl.multiple_of(h * HD, HD)
                    q = q_ref[rows, pl.ds(lanes, HD)]
                    k_t = bufs[i][pl.ds(lanes, HD), pl.ds(t * TK, TK)]
                    v = bufs[i][pl.ds(t * TK, TK), pl.ds(width + lanes, HD)]
                    s = jnp.dot(q, k_t, preferred_element_type=jnp.float32)
                    s = s * scale + bias_ref[pl.ds(i * heads + h, 1), pl.ds(t * TK, TK)]
                    s = jnp.where(valid, s, NEG_FILL)
                    m_prev = m_sc[h, rows, :]
                    m_new = jnp.maximum(m_prev, jnp.max(s, axis=1, keepdims=True))
                    p = jnp.exp(s - m_new)
                    rescale = jnp.exp(m_prev - m_new)
                    l_sc[h, rows, :] = l_sc[h, rows, :] * rescale + jnp.sum(p, axis=1, keepdims=True)
                    acc_sc[rows, pl.ds(lanes, HD)] = acc_sc[rows, pl.ds(lanes, HD)] * rescale + jnp.dot(
                        p.astype(jnp.bfloat16), v, preferred_element_type=jnp.float32
                    )
                    m_sc[h, rows, :] = m_new
                    return carry

                lax.fori_loop(0, heads, one_head, 0)

            if diag:
                body()
            else:
                pl.when(flags_ref[(qt * n_buf + i) * n_t + t] != 0)(body)
    if last:
        for h in range(heads):
            cols = pl.ds(h * HD, HD)
            ctx_ref[:, cols] = (acc_sc[:, cols] / l_sc[h]).astype(ctx_ref.dtype)
        return
    lane = lax.broadcasted_iota(jnp.int32, m_out.shape, 1)
    m_all = jnp.zeros(m_out.shape, jnp.float32)
    l_all = jnp.zeros(l_out.shape, jnp.float32)
    for h in range(heads):
        m_all = jnp.where(lane == h, m_sc[h], m_all)
        l_all = jnp.where(lane == h, l_sc[h], l_all)
    m_out[...] = m_all
    l_out[...] = l_all
    acc_out[...] = acc_sc[...]


def attention_part(state, queries, seg_q, slopes, bufs, steps_back, present, own=False, last=False):
    block_len, width = queries.shape
    heads = width // HD
    n_buf = len(bufs)
    n_q, n_t = block_len // TQ, block_len // TK
    seg_k = jnp.stack(
        [
            jnp.where(ok, buf[block_len, :block_len].astype(jnp.int32), -1)
            for buf, ok in zip(bufs, present)
        ]
    )
    if own:
        seg_k = seg_k.at[0].set(seg_q)
    seg_first = seg_q.reshape(n_q, TQ)[:, 0]
    seg_last = seg_k.reshape(n_buf, n_t, TK)[:, :, -1]
    flags = seg_last[None, :, :] >= seg_first[:, None, None]
    if own:
        earlier = jnp.arange(n_t)[None, :] < jnp.arange(n_q)[:, None]
        flags = flags.at[:, 0, :].set(flags[:, 0, :] & earlier)
    flags = flags.astype(jnp.int32).reshape(-1)
    seg_rows = jnp.concatenate(
        [seg_k, jnp.full(((-n_buf) % 8, block_len), -1, jnp.int32)], axis=0
    )
    offsets = jnp.arange(block_len, dtype=jnp.int32)
    rel = offsets[None, :] - jnp.stack(steps_back)[:, None] * block_len
    bias = (rel.astype(jnp.float32)[:, None, :] * slopes[None, :, None]).reshape(n_buf * heads, block_len)
    bias = jnp.concatenate([bias, jnp.zeros(((-n_buf * heads) % 8, block_len), jnp.float32)], axis=0)
    vmem = pl.BlockSpec(memory_space=pltpu.VMEM)
    work = heads * block_len * n_buf * block_len
    state = () if own else tuple(state)
    if last:
        out_shape = jax.ShapeDtypeStruct((block_len, width), jnp.bfloat16)
        out_specs = vmem
    else:
        out_shape = (
            jax.ShapeDtypeStruct((block_len, HD), jnp.float32),
            jax.ShapeDtypeStruct((block_len, HD), jnp.float32),
            jax.ShapeDtypeStruct((block_len, width), jnp.float32),
        )
        out_specs = (vmem, vmem, vmem)
    return pl.pallas_call(
        functools.partial(part_kernel, n_buf, own, last),
        out_shape=out_shape,
        in_specs=[pl.BlockSpec(memory_space=pltpu.SMEM)] + [vmem] * (n_buf + 4 + len(state)),
        out_specs=out_specs,
        scratch_shapes=[
            pltpu.VMEM((heads, block_len, 1), jnp.float32),
            pltpu.VMEM((heads, block_len, 1), jnp.float32),
            pltpu.VMEM((block_len, width), jnp.float32),
        ],
        cost_estimate=pl.CostEstimate(
            flops=4 * work * HD,
            transcendentals=work,
            bytes_accessed=(n_buf + 4) * block_len * width * 4,
        ),
    )(flags, queries, *bufs, seg_q.reshape(block_len, 1), seg_rows, bias, *state)

RING = 4


def moved(value, pairs):
    return lax.ppermute(value, "seq", pairs)


def relay_earlier_blocks(payload):
    count = lax.axis_size("seq")
    y = lax.axis_index("seq") % RING
    ids = range(count)
    from_z = moved(payload, [(s, s + RING) for s in ids if s + RING < count])
    from_below = moved(payload, [(s, s + 1) for s in ids if s % RING < RING - 1])
    from_wrap = moved(payload, [(s, s + RING - 1) for s in ids if s % RING == 0])
    passed_up = moved(from_below, [(s, s + 1) for s in ids if 0 < s % RING < RING - 1])
    passed_down = moved(from_z, [(s, s - 1) for s in ids if s % RING > 0])
    passed_wrap = moved(from_z, [(s, s - RING + 1) for s in ids if s % RING == RING - 1])
    passed_twice = moved(passed_down, [(s, s - 1) for s in ids if 0 < s % RING < RING - 1])
    s_now = lax.axis_index("seq")
    early = [
        (from_z, 4, s_now >= 4),
        (from_below, 1, y >= 1),
        (passed_wrap, 1, (y == 0) & (s_now >= 1)),
        (passed_down, 3, (y <= 2) & (s_now >= 3)),
        (from_wrap, 3, y == 3),
    ]
    late = [(passed_twice, 2, (y <= 1) & (s_now >= 2)), (passed_up, 2, y >= 2)]
    return early, late


def on_device(tokens, ln_gain, w_qkv, slopes, w_out, seg_ids):
    inputs = tokens.astype(jnp.float32)
    normed = layer_norm(inputs, ln_gain)
    rows_dev = normed.shape[0]
    head = lax.axis_index("head")
    n_head = lax.axis_size("head")

    width_local = w_qkv.shape[2]
    heads_dev = slopes.shape[0]
    joined = w_qkv.reshape(w_qkv.shape[0], 3 * width_local)

    def project_rows(rows):
        return jnp.dot(rows, joined, preferred_element_type=jnp.float32).astype(jnp.bfloat16)

    from_partner = swapped(normed, "head", 1)
    from_cross = swapped(normed, "head", 2)
    from_partner_cross = swapped(from_cross, "head", 1)
    near = project_rows(jnp.concatenate([normed, from_partner], axis=0))
    far = project_rows(jnp.concatenate([from_cross, from_partner_cross], axis=0))
    pieces = jnp.concatenate([near, far], axis=0).reshape(n_head, rows_dev, near.shape[1])
    qkv_rows = jnp.concatenate(
        [lax.dynamic_index_in_dim(pieces, j ^ head, 0, keepdims=False) for j in range(n_head)], axis=0
    )
    block_len = qkv_rows.shape[0]
    key_cache = qkv_rows[:, width_local : 2 * width_local]
    value_cache = qkv_rows[:, 2 * width_local :]

    kv_own = jnp.concatenate([key_cache.T, value_cache], axis=1)
    seg_row = jnp.zeros((8, kv_own.shape[1]), jnp.bfloat16).at[0, :block_len].set(
        seg_ids.astype(jnp.bfloat16)
    )
    payload = jnp.concatenate([kv_own, seg_row], axis=0)
    arrived = relay_earlier_blocks(payload)

    queries = qkv_rows[:, :width_local]
    early, late = arrived

    def unzip(entries):
        bufs, back, present = zip(*entries)
        return list(bufs), [jnp.int32(k) for k in back], list(present)

    bufs, back, present = unzip(early)
    state = attention_part(
        None, queries, seg_ids, slopes, [payload] + bufs, [jnp.int32(0)] + back,
        [jnp.bool_(True)] + present, own=True,
    )
    bufs, back, present = unzip(late)
    context = attention_part(state, queries, seg_ids, slopes, bufs, back, present, last=True)

    context4 = context.reshape(n_head, rows_dev, context.shape[1])

    def project(owners):
        rows = jnp.concatenate(
            [lax.dynamic_index_in_dim(context4, o, 0, keepdims=False) for o in owners], axis=0
        )
        out = jnp.dot(rows, w_out, preferred_element_type=jnp.float32).astype(jnp.bfloat16)
        return out.reshape(len(owners), rows_dev, w_out.shape[1])

    sent = project([head ^ 1, head ^ 3])
    kept = project([head, head ^ 2])
    chip_sum = kept.astype(jnp.float32) + swapped(sent, "head", 1).astype(jnp.float32)
    other_chip = swapped(chip_sum[1].astype(jnp.bfloat16), "head", 2).astype(jnp.float32)
    hidden = (inputs + chip_sum[0] + other_chip).astype(jnp.bfloat16)
    return (hidden, key_cache, value_cache)


def solution(mesh):
    in_specs = (
        P(("seq", "head"), None),
        P(),
        P(None, None, "head"),
        P("head"),
        P("head", None),
        P("seq"),
    )
    out_specs = (P(("seq", "head"), None), P("seq", "head"), P("seq", "head"))
    return jax.shard_map(
        on_device, mesh=mesh, in_specs=in_specs, out_specs=out_specs, check_vma=False
    )
```

```python
import functools

import jax
import jax.numpy as jnp
from jax import lax
from jax.sharding import PartitionSpec as P
from jax.experimental import pallas as pl
from jax.experimental.pallas import tpu as pltpu

HD = 128
SPAN = 4


EPSILON = 1e-05
NEG_FILL = -1e30


def shifted(value, axis, steps):
    count = lax.axis_size(axis)
    leading, last = (max(0, -steps), min(count, count - steps))
    return lax.ppermute(value, axis, [(source, source + steps) for source in range(leading, last)])


def swapped(value, axis, mask):
    count = lax.axis_size(axis)
    return lax.ppermute(value, axis, [(source, source ^ mask) for source in range(count)])


def layer_norm(inputs, ln_gain):
    row_mean = jnp.mean(inputs, axis=-1, keepdims=True)
    centred = inputs - row_mean
    variance = jnp.mean(centred * centred, axis=-1, keepdims=True)
    return (centred * lax.rsqrt(variance + EPSILON) * ln_gain).astype(jnp.bfloat16)


TQ = 256
TK = 256


def part_kernel(n_buf, own, last, flags_ref, q_ref, *refs):
    bufs = refs[:n_buf]
    segq_ref, segk_ref, bias_ref = refs[n_buf : n_buf + 3]
    rest = list(refs[n_buf + 3 :])
    if not own:
        m_in, l_in, acc_in = rest[:3]
        rest = rest[3:]
    if last:
        ctx_ref = rest.pop(0)
    else:
        m_out, l_out, acc_out = rest[:3]
        rest = rest[3:]
    m_sc, l_sc, acc_sc = rest
    heads = m_sc.shape[0]
    block_len = q_ref.shape[0]
    n_q, n_t = block_len // TQ, block_len // TK
    width = heads * HD
    scale = HD ** (-0.5)
    if own:
        m_sc[...] = jnp.full(m_sc.shape, NEG_FILL, jnp.float32)
        l_sc[...] = jnp.zeros(l_sc.shape, jnp.float32)
        acc_sc[...] = jnp.zeros(acc_sc.shape, jnp.float32)
    else:
        for h in range(heads):
            m_sc[h] = m_in[:, h : h + 1]
            l_sc[h] = l_in[:, h : h + 1]
        acc_sc[...] = acc_in[...]
    for qt in range(n_q):
        rows = pl.ds(qt * TQ, TQ)
        segq = segq_ref[rows, :]
        steps = [(i, t) for i in range(n_buf) for t in range(n_t)]
        if own:
            steps = [(0, qt)] + [(0, t) for t in range(n_t) if t * TK < qt * TQ] + steps[n_t:]
        for i, t in steps:
            diag = own and i == 0 and t == qt

            def body(i=i, t=t, diag=diag):
                valid = segq == segk_ref[pl.ds(i, 1), pl.ds(t * TK, TK)]
                if diag:
                    r = lax.broadcasted_iota(jnp.int32, (TQ, TK), 0)
                    c = lax.broadcasted_iota(jnp.int32, (TQ, TK), 1)
                    valid = valid & (c <= r)

                def one_head(h, carry):
                    lanes = pl.multiple_of(h * HD, HD)
                    q = q_ref[rows, pl.ds(lanes, HD)]
                    k_t = bufs[i][pl.ds(lanes, HD), pl.ds(t * TK, TK)]
                    v = bufs[i][pl.ds(t * TK, TK), pl.ds(width + lanes, HD)]
                    s = jnp.dot(q, k_t, preferred_element_type=jnp.float32)
                    s = s * scale + bias_ref[pl.ds(i * heads + h, 1), pl.ds(t * TK, TK)]
                    s = jnp.where(valid, s, NEG_FILL)
                    m_prev = m_sc[h, rows, :]
                    m_new = jnp.maximum(m_prev, jnp.max(s, axis=1, keepdims=True))
                    p = jnp.exp(s - m_new)
                    rescale = jnp.exp(m_prev - m_new)
                    l_sc[h, rows, :] = l_sc[h, rows, :] * rescale + jnp.sum(p, axis=1, keepdims=True)
                    acc_sc[rows, pl.ds(lanes, HD)] = acc_sc[rows, pl.ds(lanes, HD)] * rescale + jnp.dot(
                        p.astype(jnp.bfloat16), v, preferred_element_type=jnp.float32
                    )
                    m_sc[h, rows, :] = m_new
                    return carry

                lax.fori_loop(0, heads, one_head, 0, unroll=2)

            if diag:
                body()
            else:
                pl.when(flags_ref[(qt * n_buf + i) * n_t + t] != 0)(body)
    if last:
        for h in range(heads):
            cols = pl.ds(h * HD, HD)
            ctx_ref[:, cols] = (acc_sc[:, cols] / l_sc[h]).astype(ctx_ref.dtype)
        return
    lane = lax.broadcasted_iota(jnp.int32, m_out.shape, 1)
    m_all = jnp.zeros(m_out.shape, jnp.float32)
    l_all = jnp.zeros(l_out.shape, jnp.float32)
    for h in range(heads):
        m_all = jnp.where(lane == h, m_sc[h], m_all)
        l_all = jnp.where(lane == h, l_sc[h], l_all)
    m_out[...] = m_all
    l_out[...] = l_all
    acc_out[...] = acc_sc[...]


def attention_part(state, queries, seg_q, slopes, bufs, steps_back, present, own=False, last=False):
    block_len, width = queries.shape
    heads = width // HD
    n_buf = len(bufs)
    n_q, n_t = block_len // TQ, block_len // TK
    seg_k = jnp.stack(
        [
            jnp.where(ok, buf[block_len, :block_len].astype(jnp.int32), -1)
            for buf, ok in zip(bufs, present)
        ]
    )
    if own:
        seg_k = seg_k.at[0].set(seg_q)
    seg_first = seg_q.reshape(n_q, TQ)[:, 0]
    seg_last = seg_k.reshape(n_buf, n_t, TK)[:, :, -1]
    flags = seg_last[None, :, :] >= seg_first[:, None, None]
    if own:
        earlier = jnp.arange(n_t)[None, :] < jnp.arange(n_q)[:, None]
        flags = flags.at[:, 0, :].set(flags[:, 0, :] & earlier)
    flags = flags.astype(jnp.int32).reshape(-1)
    seg_rows = jnp.concatenate(
        [seg_k, jnp.full(((-n_buf) % 8, block_len), -1, jnp.int32)], axis=0
    )
    offsets = jnp.arange(block_len, dtype=jnp.int32)
    rel = offsets[None, :] - jnp.stack(steps_back)[:, None] * block_len
    bias = (rel.astype(jnp.float32)[:, None, :] * slopes[None, :, None]).reshape(n_buf * heads, block_len)
    bias = jnp.concatenate([bias, jnp.zeros(((-n_buf * heads) % 8, block_len), jnp.float32)], axis=0)
    vmem = pl.BlockSpec(memory_space=pltpu.VMEM)
    work = heads * block_len * n_buf * block_len
    state = () if own else tuple(state)
    if last:
        out_shape = jax.ShapeDtypeStruct((block_len, width), jnp.bfloat16)
        out_specs = vmem
    else:
        out_shape = (
            jax.ShapeDtypeStruct((block_len, HD), jnp.float32),
            jax.ShapeDtypeStruct((block_len, HD), jnp.float32),
            jax.ShapeDtypeStruct((block_len, width), jnp.float32),
        )
        out_specs = (vmem, vmem, vmem)
    return pl.pallas_call(
        functools.partial(part_kernel, n_buf, own, last),
        out_shape=out_shape,
        in_specs=[pl.BlockSpec(memory_space=pltpu.SMEM)] + [vmem] * (n_buf + 4 + len(state)),
        out_specs=out_specs,
        scratch_shapes=[
            pltpu.VMEM((heads, block_len, 1), jnp.float32),
            pltpu.VMEM((heads, block_len, 1), jnp.float32),
            pltpu.VMEM((block_len, width), jnp.float32),
        ],
        cost_estimate=pl.CostEstimate(
            flops=4 * work * HD,
            transcendentals=work,
            bytes_accessed=(n_buf + 4) * block_len * width * 4,
        ),
    )(flags, queries, *bufs, seg_q.reshape(block_len, 1), seg_rows, bias, *state)

RING = 4


def moved(value, pairs):
    return lax.ppermute(value, "seq", pairs)


def relay_earlier_blocks(payload):
    count = lax.axis_size("seq")
    y = lax.axis_index("seq") % RING
    ids = range(count)
    from_z = moved(payload, [(s, s + RING) for s in ids if s + RING < count])
    from_below = moved(payload, [(s, s + 1) for s in ids if s % RING < RING - 1])
    from_wrap = moved(payload, [(s, s + RING - 1) for s in ids if s % RING == 0])
    passed_up = moved(from_below, [(s, s + 1) for s in ids if 0 < s % RING < RING - 1])
    passed_down = moved(from_z, [(s, s - 1) for s in ids if s % RING > 0])
    passed_wrap = moved(from_z, [(s, s - RING + 1) for s in ids if s % RING == RING - 1])
    passed_twice = moved(passed_down, [(s, s - 1) for s in ids if 0 < s % RING < RING - 1])
    back1 = jnp.where(y == 0, passed_wrap, from_below)
    back2 = jnp.where(y <= 1, passed_twice, passed_up)
    back3 = jnp.where(y <= 2, passed_down, from_wrap)
    return [back1, back2, back3, from_z]


def on_device(tokens, ln_gain, w_qkv, slopes, w_out, seg_ids):
    inputs = tokens.astype(jnp.float32)
    normed = layer_norm(inputs, ln_gain)
    rows_dev = normed.shape[0]
    head = lax.axis_index("head")
    n_head = lax.axis_size("head")

    width_local = w_qkv.shape[2]
    heads_dev = slopes.shape[0]
    joined = w_qkv.reshape(w_qkv.shape[0], 3 * width_local)

    def project_rows(rows):
        return jnp.dot(rows, joined, preferred_element_type=jnp.float32).astype(jnp.bfloat16)

    from_partner = swapped(normed, "head", 1)
    from_cross = swapped(normed, "head", 2)
    from_partner_cross = swapped(from_cross, "head", 1)
    near = project_rows(jnp.concatenate([normed, from_partner], axis=0))
    far = project_rows(jnp.concatenate([from_cross, from_partner_cross], axis=0))
    pieces = jnp.concatenate([near, far], axis=0).reshape(n_head, rows_dev, near.shape[1])
    qkv_rows = jnp.concatenate(
        [lax.dynamic_index_in_dim(pieces, j ^ head, 0, keepdims=False) for j in range(n_head)], axis=0
    )
    block_len = qkv_rows.shape[0]
    key_cache = qkv_rows[:, width_local : 2 * width_local]
    value_cache = qkv_rows[:, 2 * width_local :]

    kv_own = jnp.concatenate([key_cache.T, value_cache], axis=1)
    seg_row = jnp.zeros((8, kv_own.shape[1]), jnp.bfloat16).at[0, :block_len].set(
        seg_ids.astype(jnp.bfloat16)
    )
    payload = jnp.concatenate([kv_own, seg_row], axis=0)
    arrived = relay_earlier_blocks(payload)

    queries = qkv_rows[:, :width_local]
    back1, back2, back3, from_z = arrived
    seq_index_now = lax.axis_index("seq")
    state = attention_part(
        None,
        queries,
        seg_ids,
        slopes,
        [payload, from_z, back1, back3],
        [jnp.int32(0), jnp.int32(4), jnp.int32(1), jnp.int32(3)],
        [jnp.bool_(True), seq_index_now >= 4, seq_index_now >= 1, seq_index_now >= 3],
        own=True,
    )
    context = attention_part(
        state, queries, seg_ids, slopes, [back2], [jnp.int32(2)], [seq_index_now >= 2], last=True
    )

    context4 = context.reshape(n_head, rows_dev, context.shape[1])

    def project(owners):
        rows = jnp.concatenate(
            [lax.dynamic_index_in_dim(context4, o, 0, keepdims=False) for o in owners], axis=0
        )
        out = jnp.dot(rows, w_out, preferred_element_type=jnp.float32).astype(jnp.bfloat16)
        return out.reshape(len(owners), rows_dev, w_out.shape[1])

    sent = project([head ^ 1, head ^ 3])
    kept = project([head, head ^ 2])
    chip_sum = kept.astype(jnp.float32) + swapped(sent, "head", 1).astype(jnp.float32)
    other_chip = swapped(chip_sum[1].astype(jnp.bfloat16), "head", 2).astype(jnp.float32)
    hidden = (inputs + chip_sum[0] + other_chip).astype(jnp.bfloat16)
    return (hidden, key_cache, value_cache)


def solution(mesh):
    in_specs = (
        P(("seq", "head"), None),
        P(),
        P(None, None, "head"),
        P("head"),
        P("head", None),
        P("seq"),
    )
    out_specs = (P(("seq", "head"), None), P("seq", "head"), P("seq", "head"))
    return jax.shard_map(
        on_device, mesh=mesh, in_specs=in_specs, out_specs=out_specs, check_vma=False
    )
```

```python
import functools

import jax
import jax.numpy as jnp
from jax import lax
from jax.sharding import PartitionSpec as P
from jax.experimental import pallas as pl
from jax.experimental.pallas import tpu as pltpu

HD = 128
SPAN = 4


EPSILON = 1e-05
NEG_FILL = -1e30


def shifted(value, axis, steps):
    count = lax.axis_size(axis)
    leading, last = (max(0, -steps), min(count, count - steps))
    return lax.ppermute(value, axis, [(source, source + steps) for source in range(leading, last)])


def swapped(value, axis, mask):
    count = lax.axis_size(axis)
    return lax.ppermute(value, axis, [(source, source ^ mask) for source in range(count)])


def layer_norm(inputs, ln_gain):
    row_mean = jnp.mean(inputs, axis=-1, keepdims=True)
    centred = inputs - row_mean
    variance = jnp.mean(centred * centred, axis=-1, keepdims=True)
    return (centred * lax.rsqrt(variance + EPSILON) * ln_gain).astype(jnp.bfloat16)


TQ = 256
TK = 256


def part_kernel(n_buf, own, last, flags_ref, q_ref, *refs):
    bufs = refs[:n_buf]
    segq_ref, segk_ref, bias_ref = refs[n_buf : n_buf + 3]
    rest = list(refs[n_buf + 3 :])
    if not own:
        m_in, l_in, acc_in = rest[:3]
        rest = rest[3:]
    if last:
        ctx_ref = rest.pop(0)
    else:
        m_out, l_out, acc_out = rest[:3]
        rest = rest[3:]
    m_sc, l_sc, acc_sc = rest
    heads = m_sc.shape[0]
    block_len = q_ref.shape[0]
    n_q, n_t = block_len // TQ, block_len // TK
    width = heads * HD
    scale = HD ** (-0.5)
    if own:
        m_sc[...] = jnp.full(m_sc.shape, NEG_FILL, jnp.float32)
        l_sc[...] = jnp.zeros(l_sc.shape, jnp.float32)
        acc_sc[...] = jnp.zeros(acc_sc.shape, jnp.float32)
    else:
        for h in range(heads):
            m_sc[h] = m_in[:, h : h + 1]
            l_sc[h] = l_in[:, h : h + 1]
        acc_sc[...] = acc_in[...]
    for qt in range(n_q):
        rows = pl.ds(qt * TQ, TQ)
        segq = segq_ref[rows, :]
        steps = [(i, t) for i in range(n_buf) for t in range(n_t)]
        if own:
            steps = [(0, qt)] + [(0, t) for t in range(n_t) if t * TK < qt * TQ] + steps[n_t:]
        for i, t in steps:
            diag = own and i == 0 and t == qt

            def body(i=i, t=t, diag=diag):
                valid = segq == segk_ref[pl.ds(i, 1), pl.ds(t * TK, TK)]
                if diag:
                    r = lax.broadcasted_iota(jnp.int32, (TQ, TK), 0)
                    c = lax.broadcasted_iota(jnp.int32, (TQ, TK), 1)
                    valid = valid & (c <= r)

                def one_head(h, carry):
                    lanes = pl.multiple_of(h * HD, HD)
                    q = q_ref[rows, pl.ds(lanes, HD)]
                    k_t = bufs[i][pl.ds(lanes, HD), pl.ds(t * TK, TK)]
                    v = bufs[i][pl.ds(t * TK, TK), pl.ds(width + lanes, HD)]
                    s = jnp.dot(q, k_t, preferred_element_type=jnp.float32)
                    s = s * scale + bias_ref[pl.ds(i * heads + h, 1), pl.ds(t * TK, TK)]
                    s = jnp.where(valid, s, NEG_FILL)
                    m_prev = m_sc[h, rows, :]
                    m_new = jnp.maximum(m_prev, jnp.max(s, axis=1, keepdims=True))
                    p = jnp.exp(s - m_new)
                    rescale = jnp.exp(m_prev - m_new)
                    l_sc[h, rows, :] = l_sc[h, rows, :] * rescale + jnp.sum(p, axis=1, keepdims=True)
                    acc_sc[rows, pl.ds(lanes, HD)] = acc_sc[rows, pl.ds(lanes, HD)] * rescale + jnp.dot(
                        p.astype(jnp.bfloat16), v, preferred_element_type=jnp.float32
                    )
                    m_sc[h, rows, :] = m_new
                    return carry

                lax.fori_loop(0, heads, one_head, 0)

            if diag:
                body()
            else:
                pl.when(flags_ref[(qt * n_buf + i) * n_t + t] != 0)(body)
    if last:
        for h in range(heads):
            cols = pl.ds(h * HD, HD)
            ctx_ref[:, cols] = (acc_sc[:, cols] / l_sc[h]).astype(ctx_ref.dtype)
        return
    lane = lax.broadcasted_iota(jnp.int32, m_out.shape, 1)
    m_all = jnp.zeros(m_out.shape, jnp.float32)
    l_all = jnp.zeros(l_out.shape, jnp.float32)
    for h in range(heads):
        m_all = jnp.where(lane == h, m_sc[h], m_all)
        l_all = jnp.where(lane == h, l_sc[h], l_all)
    m_out[...] = m_all
    l_out[...] = l_all
    acc_out[...] = acc_sc[...]


def attention_part(state, queries, seg_q, slopes, bufs, steps_back, present, own=False, last=False):
    block_len, width = queries.shape
    heads = width // HD
    n_buf = len(bufs)
    n_q, n_t = block_len // TQ, block_len // TK
    seg_k = jnp.stack(
        [
            jnp.where(ok, buf[block_len, :block_len].astype(jnp.int32), -1)
            for buf, ok in zip(bufs, present)
        ]
    )
    if own:
        seg_k = seg_k.at[0].set(seg_q)
    seg_first = seg_q.reshape(n_q, TQ)[:, 0]
    seg_last = seg_k.reshape(n_buf, n_t, TK)[:, :, -1]
    flags = seg_last[None, :, :] >= seg_first[:, None, None]
    if own:
        earlier = jnp.arange(n_t)[None, :] < jnp.arange(n_q)[:, None]
        flags = flags.at[:, 0, :].set(flags[:, 0, :] & earlier)
    flags = flags.astype(jnp.int32).reshape(-1)
    seg_rows = jnp.concatenate(
        [seg_k, jnp.full(((-n_buf) % 8, block_len), -1, jnp.int32)], axis=0
    )
    offsets = jnp.arange(block_len, dtype=jnp.int32)
    rel = offsets[None, :] - jnp.stack(steps_back)[:, None] * block_len
    bias = (rel.astype(jnp.float32)[:, None, :] * slopes[None, :, None]).reshape(n_buf * heads, block_len)
    bias = jnp.concatenate([bias, jnp.zeros(((-n_buf * heads) % 8, block_len), jnp.float32)], axis=0)
    vmem = pl.BlockSpec(memory_space=pltpu.VMEM)
    work = heads * block_len * n_buf * block_len
    state = () if own else tuple(state)
    if last:
        out_shape = jax.ShapeDtypeStruct((block_len, width), jnp.bfloat16)
        out_specs = vmem
    else:
        out_shape = (
            jax.ShapeDtypeStruct((block_len, HD), jnp.float32),
            jax.ShapeDtypeStruct((block_len, HD), jnp.float32),
            jax.ShapeDtypeStruct((block_len, width), jnp.float32),
        )
        out_specs = (vmem, vmem, vmem)
    return pl.pallas_call(
        functools.partial(part_kernel, n_buf, own, last),
        out_shape=out_shape,
        in_specs=[pl.BlockSpec(memory_space=pltpu.SMEM)] + [vmem] * (n_buf + 4 + len(state)),
        out_specs=out_specs,
        scratch_shapes=[
            pltpu.VMEM((heads, block_len, 1), jnp.float32),
            pltpu.VMEM((heads, block_len, 1), jnp.float32),
            pltpu.VMEM((block_len, width), jnp.float32),
        ],
        cost_estimate=pl.CostEstimate(
            flops=4 * work * HD,
            transcendentals=work,
            bytes_accessed=(n_buf + 4) * block_len * width * 4,
        ),
    )(flags, queries, *bufs, seg_q.reshape(block_len, 1), seg_rows, bias, *state)

RING = 4


def moved(value, pairs):
    return lax.ppermute(value, "seq", pairs)


def relay_earlier_blocks(payload):
    count = lax.axis_size("seq")
    y = lax.axis_index("seq") % RING
    ids = range(count)
    from_z = moved(payload, [(s, s + RING) for s in ids if s + RING < count])
    from_below = moved(payload, [(s, s + 1) for s in ids if s % RING < RING - 1])
    from_wrap = moved(payload, [(s, s + RING - 1) for s in ids if s % RING == 0])
    passed_up = moved(from_below, [(s, s + 1) for s in ids if 0 < s % RING < RING - 1])
    passed_down = moved(from_z, [(s, s - 1) for s in ids if s % RING > 0])
    passed_wrap = moved(from_z, [(s, s - RING + 1) for s in ids if s % RING == RING - 1])
    passed_twice = moved(passed_down, [(s, s - 1) for s in ids if 0 < s % RING < RING - 1])
    back1 = jnp.where(y == 0, passed_wrap, from_below)
    s_now = lax.axis_index("seq")
    late = [(passed_twice, 2, (y <= 1) & (s_now >= 2)), (passed_up, 2, y >= 2)]
    back3 = jnp.where(y <= 2, passed_down, from_wrap)
    return [back1, late, back3, from_z]


def on_device(tokens, ln_gain, w_qkv, slopes, w_out, seg_ids):
    inputs = tokens.astype(jnp.float32)
    normed = layer_norm(inputs, ln_gain)
    rows_dev = normed.shape[0]
    head = lax.axis_index("head")
    n_head = lax.axis_size("head")

    width_local = w_qkv.shape[2]
    heads_dev = slopes.shape[0]
    joined = w_qkv.reshape(w_qkv.shape[0], 3 * width_local)

    def project_rows(rows):
        return jnp.dot(rows, joined, preferred_element_type=jnp.float32).astype(jnp.bfloat16)

    from_partner = swapped(normed, "head", 1)
    from_cross = swapped(normed, "head", 2)
    from_partner_cross = swapped(from_cross, "head", 1)
    near = project_rows(jnp.concatenate([normed, from_partner], axis=0))
    far = project_rows(jnp.concatenate([from_cross, from_partner_cross], axis=0))
    pieces = jnp.concatenate([near, far], axis=0).reshape(n_head, rows_dev, near.shape[1])
    qkv_rows = jnp.concatenate(
        [lax.dynamic_index_in_dim(pieces, j ^ head, 0, keepdims=False) for j in range(n_head)], axis=0
    )
    block_len = qkv_rows.shape[0]
    key_cache = qkv_rows[:, width_local : 2 * width_local]
    value_cache = qkv_rows[:, 2 * width_local :]

    kv_own = jnp.concatenate([key_cache.T, value_cache], axis=1)
    seg_row = jnp.zeros((8, kv_own.shape[1]), jnp.bfloat16).at[0, :block_len].set(
        seg_ids.astype(jnp.bfloat16)
    )
    payload = jnp.concatenate([kv_own, seg_row], axis=0)
    arrived = relay_earlier_blocks(payload)

    queries = qkv_rows[:, :width_local]
    back1, back2, back3, from_z = arrived
    seq_index_now = lax.axis_index("seq")
    state = attention_part(
        None,
        queries,
        seg_ids,
        slopes,
        [payload, from_z, back1, back3],
        [jnp.int32(0), jnp.int32(4), jnp.int32(1), jnp.int32(3)],
        [jnp.bool_(True), seq_index_now >= 4, seq_index_now >= 1, seq_index_now >= 3],
        own=True,
    )
    late_bufs, late_back, late_present = zip(*back2)
    context = attention_part(
        state, queries, seg_ids, slopes, list(late_bufs), [jnp.int32(k) for k in late_back],
        list(late_present), last=True,
    )

    context4 = context.reshape(n_head, rows_dev, context.shape[1])

    def project(owners):
        rows = jnp.concatenate(
            [lax.dynamic_index_in_dim(context4, o, 0, keepdims=False) for o in owners], axis=0
        )
        out = jnp.dot(rows, w_out, preferred_element_type=jnp.float32).astype(jnp.bfloat16)
        return out.reshape(len(owners), rows_dev, w_out.shape[1])

    sent = project([head ^ 1, head ^ 3])
    kept = project([head, head ^ 2])
    chip_sum = kept.astype(jnp.float32) + swapped(sent, "head", 1).astype(jnp.float32)
    other_chip = swapped(chip_sum[1].astype(jnp.bfloat16), "head", 2).astype(jnp.float32)
    hidden = (inputs + chip_sum[0] + other_chip).astype(jnp.bfloat16)
    return (hidden, key_cache, value_cache)


def solution(mesh):
    in_specs = (
        P(("seq", "head"), None),
        P(),
        P(None, None, "head"),
        P("head"),
        P("head", None),
        P("seq"),
    )
    out_specs = (P(("seq", "head"), None), P("seq", "head"), P("seq", "head"))
    return jax.shard_map(
        on_device, mesh=mesh, in_specs=in_specs, out_specs=out_specs, check_vma=False
    )
```
